512 devices in a mesh: space: 64 (over y_lo, z, core), band: 8 (over y_hi, x).
Axes of the slice: x: 4, y: 8 (y_hi: 2, y_lo: 4; y = y_hi * 4 + y_lo), z: 8, core: 2. Of those that a mesh axis runs over, the one named last changes fastest.
Arguments:
- bands: bfloat16 [16, 4, 128, 128, 128], P('band', None, 'space'), may hold values from -6 to 6
- occ_level: int32 [16], P('band'), may hold values from 1 to 4
- block_owner: int32 [1], replicated, may hold values from 0 to 15
Outputs:
- exchange: float32 [2, 4, 128, 128, 128], P(None, None, 'space', 'band')
The draws below stay inside these ranges and needn't reach their ends.
All inputs are finite; a program needn't handle non-finite values.
Results may differ from the reference program's by a relative error of at most 0.0013.
Values may be sent and summed in bfloat16 or wider, within the bound.
No kernel may reach another device: no remote copies, remote signals or barrier semaphores. Data moves between devices by JAX's collectives and lax.ppermute only.
A program may use at most 64 MiB of HBM per device.

```python
import jax
import jax.numpy as jnp
from jax import lax

NX = 128
NY = 128
RES_DEV = 2
BLOCK = 2
SWEEPS = 4
NZ = 128
BANDS = 16


def place_ends(array, rng, low, largest):
    longest = array.shape.index(max(array.shape))
    spots = []
    for shift in (0, 1):
        where = [jax.random.randint(jax.random.fold_in(rng, axis), (), 0, length) for axis, length in enumerate(array.shape)]
        where[longest] = (where[longest] + shift) % array.shape[longest]
        spots.append(tuple(where))
    return array.at[spots[0]].set(low).at[spots[1]].set(largest)


def levels(own_key, shape, pieces, least, high):
    factor_of, own = 1.0, jax.random.fold_in(own_key, 6)
    for axis_at, blocks in pieces:
        steps = jnp.exp(jax.random.uniform(jax.random.fold_in(own, axis_at), (blocks,), jnp.float32, least / len(pieces), high / len(pieces)))
        factor_of = factor_of * jnp.repeat(steps, shape[axis_at] // blocks).reshape([-1 if axis == axis_at else 1 for axis in range(len(shape))])
    return factor_of


def gaussian(rng, dims, width, most, shards=(), held_as=jnp.bfloat16):
    values = jax.random.normal(rng, dims, jnp.float32) * width
    if len(shards) > 0:
        values = levels(rng, dims, shards, -0.22, 0.18) * values
    return jnp.clip(values, min=-most, max=most).astype(held_as)


def setup_inputs(seed: int = 0) -> dict:
    key_of = jax.random.split(jax.random.key(seed), 4)
    return {
        "bands": gaussian(key_of[0], (BANDS, 4, NZ, NX, NY), 1.0, 6.0, ((0, 8), (2, 64))),
        "occ_level": place_ends(jax.random.randint(key_of[1], (BANDS,), 1, 5), jax.random.fold_in(key_of[1], 1), 1, 4).astype(jnp.int32),
        "block_owner": jax.random.randint(key_of[2], (1,), 0, BANDS).astype(jnp.int32),
    }


jacobi_diagonal = 6.5

def relax_field(density):
    field = density / jacobi_diagonal
    for sweep_index in range(SWEEPS - 1):
        beside = jnp.roll(field, 1, -3) + jnp.roll(field, -1, -3)
        beside = beside + jnp.roll(field, 1, -2) + jnp.roll(field, -1, -2)
        beside = beside + jnp.roll(field, 1, -1) + jnp.roll(field, -1, -1)
        field = (density + beside) / jacobi_diagonal
    return field

def reference(bands, occ_level, block_owner):
    first = block_owner[0].astype(jnp.int32)
    group = first // RES_DEV
    offset = first % RES_DEV
    picks = group * RES_DEV + (offset + jnp.arange(BLOCK, dtype=jnp.int32)) % RES_DEV
    block = jnp.take(bands, picks.astype(jnp.int32), axis=0).astype(jnp.float32)

    def one_band(total, item):
        orbital, level = item
        orbital = orbital.astype(jnp.float32)
        dens_real = orbital[0] * block[:, 0] + orbital[1] * block[:, 1] + orbital[2] * block[:, 2] + orbital[3] * block[:, 3]
        dens_imag = orbital[0] * block[:, 1] - orbital[1] * block[:, 0] + orbital[2] * block[:, 3] - orbital[3] * block[:, 2]
        pot_real = relax_field(dens_real)
        pot_imag = relax_field(dens_imag)
        weight = level.astype(jnp.float32) * 0.25
        parts = []
        for spin in range(2):
            parts.append(orbital[2 * spin] * pot_real - orbital[2 * spin + 1] * pot_imag)
            parts.append(orbital[2 * spin] * pot_imag + orbital[2 * spin + 1] * pot_real)
        return (total + weight * jnp.stack(parts, axis=1), None)
    initial = jnp.zeros((BLOCK, 4) + bands.shape[2:], jnp.float32)
    total, unused = lax.scan(one_band, initial, (bands, occ_level))
    return -(1.0 / jnp.sqrt(jnp.float32(BANDS))) * total
```

```python
import jax
import jax.numpy as jnp
from jax import lax
from jax.experimental import pallas as pl
from jax.experimental.pallas import tpu as pltpu
from jax.sharding import PartitionSpec as P

SWEEPS = 4
jacobi_diagonal = 6.5

H = SWEEPS - 1
RES = 2
COMPS = 4
PLANES = 2
LANES = 128
GROUPS = 8
ROWS = 16
WIN = ROWS + 2 * H
BODY = PLANES * RES * COMPS * WIN
SEND = BODY + 8
F32 = jnp.float32
BF16 = jnp.bfloat16

def rows_of(d):
    return d, WIN - d


def plane_row(p, k, c):
    return ((p * RES + k) * COMPS + c) * WIN


N1 = RES * COMPS * ((WIN - 2) + (WIN - 4))
N2 = RES * COMPS * (WIN - 6)


def near_row(k, c):
    return (k * COMPS + c) * (WIN - 2)


def mid_row(k, c):
    return RES * COMPS * (WIN - 2) + (k * COMPS + c) * (WIN - 4)


def far_row(k, c):
    return (k * COMPS + c) * (WIN - 6)


def pack_kernel(bands_ref, occ_ref, out_ref, ext, flat):
    x = bands_ref.shape[1]
    for p in range(PLANES):
        for k in range(RES):
            for c in range(COMPS):
                n = (p * RES + k) * COMPS + c
                t = bands_ref[(k * COMPS + c) * PLANES + p].astype(F32)
                ext[n, 8:8 + x] = t
                ext[n, 0:8] = t[x - 8:x]
                ext[n, 8 + x:16 + x] = t[0:8]
    for k in range(RES):
        flat[BODY + 4 * k:BODY + 4 * k + 4] = jnp.full((4, LANES), occ_ref[k].astype(F32), F32)
    for b in range(GROUPS):
        for n in range(PLANES * RES * COMPS):
            flat[n * WIN:(n + 1) * WIN] = ext[n, ROWS * b + 8 - H:ROWS * b + 8 - H + WIN]
        out_ref[b] = flat[...].astype(BF16)


def cut_kernel(own_ref, up1_ref, dn1_ref, up2_ref, dn2_ref, flat, s1, s2, s3, s4):
    def one(src, carry):
        flat[...] = own_ref[src].astype(F32)
        for k in range(RES):
            for c in range(COMPS):
                for near, far, st1, st2 in ((1, 0, s1, s3), (0, 1, s2, s4)):
                    a = plane_row(near, k, c)
                    o = plane_row(far, k, c)
                    q = near_row(k, c)
                    st1[q:q + WIN - 2] = flat[a + 1:a + WIN - 1]
                    q = mid_row(k, c)
                    st1[q:q + WIN - 4] = flat[o + 2:o + WIN - 2]
                    q = far_row(k, c)
                    st2[q:q + WIN - 6] = flat[a + 3:a + WIN - 3]
        up1_ref[src] = s1[...].astype(BF16)
        dn1_ref[src] = s2[...].astype(BF16)
        up2_ref[src] = s3[...].astype(BF16)
        dn2_ref[src] = s4[...].astype(BF16)
        return carry
    lax.fori_loop(0, GROUPS, one, 0)


def starts_of(lo, hi):
    out = list(range(lo, hi - 7, 8))
    if out[-1] + 8 < hi:
        out.append(hi - 8)
    return out


def relax_kernel(owner_ref, own_ref, a1_ref, b1_ref, a2_ref, b2_ref, out_ref,
                 f0, fa1, fb1, fa2, fb2, blk, den, w2, w3):
    cc = 1.0 / jacobi_diagonal

    def widen(src, carry):
        f0[src] = own_ref[src].astype(F32)
        fa1[src] = a1_ref[src].astype(F32)
        fb1[src] = b1_ref[src].astype(F32)
        fa2[src] = a2_ref[src].astype(F32)
        fb2[src] = b2_ref[src].astype(F32)
        return carry
    lax.fori_loop(0, GROUPS, widen, 0)

    def span(z):
        return rows_of(max(H - z, z - H - 1, 0))

    def field(src, k, c, z, r):
        if z == 3 or z == 4:
            q = plane_row(z - 3, k, c) + r
            return f0[src, q:q + 8]
        if z == 2 or z == 5:
            q = near_row(k, c) + r - 1
            return (fa1 if z == 2 else fb1)[src, q:q + 8]
        if z == 1 or z == 6:
            q = mid_row(k, c) + r - 2
            return (fa1 if z == 1 else fb1)[src, q:q + 8]
        q = far_row(k, c) + r - 3
        return (fa2 if z == 0 else fb2)[src, q:q + 8]

    first = owner_ref[0]
    group = first // RES
    swap = (first % RES) == 1
    for z in range(8):
        lo, hi = span(z)
        for r in starts_of(lo, hi):
            for c in range(COMPS):
                t0 = field(group, 0, c, z, r)
                t1 = field(group, 1, c, z, r)
                blk[0, z, c, r:r + 8] = jnp.where(swap, t1, t0)
                blk[1, z, c, r:r + 8] = jnp.where(swap, t0, t1)

    out_ref[...] = jnp.zeros(out_ref.shape, F32)

    def around(ref, q, z, zo, r):
        here = ref[q, z - zo, r:r + 8]
        t = ref[q, z - zo - 1, r:r + 8] + ref[q, z - zo + 1, r:r + 8]
        t = t + (ref[q, z - zo, r - 1:r + 7] + ref[q, z - zo, r + 1:r + 9])
        return t + (pltpu.roll(here, 1, 1) + pltpu.roll(here, LANES - 1, 1))

    def one_group(src, carry):
        for k in range(RES):
            for z in range(8):
                lo, hi = span(z)
                for r in starts_of(lo, hi):
                    a = [field(src, k, c, z, r) for c in range(COMPS)]
                    for j in range(RES):
                        b = [blk[j, z, c, r:r + 8] for c in range(COMPS)]
                        den[2 * j, z, r:r + 8] = (a[0] * b[0] + a[1] * b[1]) + (a[2] * b[2] + a[3] * b[3])
                        den[2 * j + 1, z, r:r + 8] = (a[0] * b[1] - a[1] * b[0]) + (a[2] * b[3] - a[3] * b[2])
            for q in range(2 * RES):
                for z in range(1, 7):
                    lo, hi = span(z)
                    for r in starts_of(lo + 1, hi - 1):
                        w2[q, z - 1, r:r + 8] = den[q, z, r:r + 8] + cc * around(den, q, z, 0, r)
                for z in range(2, 6):
                    lo, hi = span(z)
                    for r in starts_of(lo + 2, hi - 2):
                        w3[q, z - 2, r:r + 8] = den[q, z, r:r + 8] + cc * around(w2, q, z, 1, r)
            scale = f0[src, BODY + 4 * k:BODY + 4 * k + 1] * (-0.25 * 0.25 * cc)
            scale = jnp.broadcast_to(scale, (8, LANES))
            for z in range(3, 5):
                for r in starts_of(H, H + ROWS):
                    a = [field(src, k, c, z, r) for c in range(COMPS)]
                    for j in range(RES):
                        v = [scale * (den[q, z, r:r + 8] + cc * around(w3, q, z, 2, r)) for q in (2 * j, 2 * j + 1)]
                        for s in range(2):
                            o = r - H
                            out_ref[j, 2 * s, z - 3, o:o + 8] += a[2 * s] * v[0] - a[2 * s + 1] * v[1]
                            out_ref[j, 2 * s + 1, z - 3, o:o + 8] += a[2 * s] * v[1] + a[2 * s + 1] * v[0]
        return carry
    lax.fori_loop(0, GROUPS, one_group, 0)


INTERPRET = False


def on_device(bands, occ_level, block_owner):
    smem = pl.BlockSpec(memory_space=pltpu.SMEM)
    vmem = pl.BlockSpec(memory_space=pltpu.VMEM)
    x = bands.shape[3]
    send = pl.pallas_call(
        pack_kernel,
        out_shape=jax.ShapeDtypeStruct((GROUPS, SEND, LANES), BF16),
        in_specs=[vmem, smem], out_specs=vmem,
        scratch_shapes=[pltpu.VMEM((PLANES * RES * COMPS, x + 16, LANES), F32), pltpu.VMEM((SEND, LANES), F32)],
        interpret=INTERPRET, name="pack",
    )(bands.reshape(RES * COMPS * PLANES, x, LANES), occ_level)
    own = lax.all_to_all(send, "band", 0, 0, tiled=True)

    up1, dn1, up2, dn2 = pl.pallas_call(
        cut_kernel,
        out_shape=[jax.ShapeDtypeStruct((GROUPS, n, LANES), BF16) for n in (N1, N1, N2, N2)],
        in_specs=[vmem], out_specs=[vmem] * 4,
        scratch_shapes=[pltpu.VMEM((n, LANES), F32) for n in (SEND, N1, N1, N2, N2)],
        interpret=INTERPRET, name="cut",
    )(own)
    count = lax.axis_size("space")

    def shift(value, by):
        return lax.ppermute(value, "space", [(i, (i + by) % count) for i in range(count)])

    below1 = shift(up1, 1)
    above1 = shift(dn1, -1)
    below2 = shift(up2, 2)
    above2 = shift(dn2, -2)

    return pl.pallas_call(
        relax_kernel,
        out_shape=jax.ShapeDtypeStruct((RES, COMPS, PLANES, ROWS, LANES), F32),
        in_specs=[smem] + [vmem] * 5, out_specs=vmem,
        scratch_shapes=[pltpu.VMEM((GROUPS, n, LANES), F32) for n in (SEND, N1, N1, N2, N2)] + [
            pltpu.VMEM((RES, 8, COMPS, 24, LANES), F32),
            pltpu.VMEM((2 * RES, 8, 24, LANES), F32),
            pltpu.VMEM((2 * RES, 6, 24, LANES), F32),
            pltpu.VMEM((2 * RES, 4, 24, LANES), F32)],
        interpret=INTERPRET, name="relax",
    )(block_owner, own, below1, above1, below2, above2)


def solution(mesh):
    return jax.shard_map(
        on_device,
        mesh=mesh,
        in_specs=(P("band", None, "space", None, None), P("band"), P()),
        out_specs=P(None, None, "space", "band", None),
        check_vma=False,
    )
```

```python
import jax
import jax.numpy as jnp
from jax import lax
from jax.experimental import pallas as pl
from jax.experimental.pallas import tpu as pltpu
from jax.sharding import PartitionSpec as P

SWEEPS = 4
jacobi_diagonal = 6.5

H = SWEEPS - 1
RES = 2
COMPS = 4
PLANES = 2
LANES = 128
GROUPS = 8
ROWS = 16
WIN = ROWS + 2 * H
BODY = PLANES * RES * COMPS * WIN
SEND = BODY + 8
F32 = jnp.float32
BF16 = jnp.bfloat16

def rows_of(d):
    return d, WIN - d


def plane_row(p, k, c):
    return ((p * RES + k) * COMPS + c) * WIN


N1 = RES * COMPS * ((WIN - 2) + (WIN - 4))
N2 = RES * COMPS * (WIN - 6)


def near_row(k, c):
    return (k * COMPS + c) * (WIN - 2)


def mid_row(k, c):
    return RES * COMPS * (WIN - 2) + (k * COMPS + c) * (WIN - 4)


def far_row(k, c):
    return (k * COMPS + c) * (WIN - 6)


def pack_kernel(core_ref, bands_ref, occ_ref, out_ref, ext, flat):
    x = bands_ref.shape[1]
    core = core_ref[0]
    for p in range(PLANES):
        plane = core if p == 0 else 1 - core
        for k in range(RES):
            for c in range(COMPS):
                n = (p * RES + k) * COMPS + c
                t = bands_ref[(k * COMPS + c) * PLANES + plane].astype(F32)
                ext[n, 8:8 + x] = t
                ext[n, 0:8] = t[x - 8:x]
                ext[n, 8 + x:16 + x] = t[0:8]
    for k in range(RES):
        flat[BODY + 4 * k:BODY + 4 * k + 4] = jnp.full((4, LANES), occ_ref[k].astype(F32), F32)
    for b in range(GROUPS):
        for n in range(PLANES * RES * COMPS):
            flat[n * WIN:(n + 1) * WIN] = ext[n, ROWS * b + 8 - H:ROWS * b + 8 - H + WIN]
        out_ref[b] = flat[...].astype(BF16)


def cut_kernel(own_ref, wide_ref, in1_ref, out3_ref, in3_ref, out1_ref, s1, s3, s4, s2):
    def one(src, carry):
        wide_ref[src] = own_ref[src].astype(F32)
        for k in range(RES):
            for c in range(COMPS):
                a = plane_row(0, k, c)
                o = plane_row(1, k, c)
                q = near_row(k, c)
                s1[q:q + WIN - 2] = wide_ref[src, o + 1:o + WIN - 1]
                s2[q:q + WIN - 2] = wide_ref[src, a + 1:a + WIN - 1]
                q = mid_row(k, c)
                s1[q:q + WIN - 4] = wide_ref[src, a + 2:a + WIN - 2]
                s2[q:q + WIN - 4] = wide_ref[src, o + 2:o + WIN - 2]
                q = far_row(k, c)
                s3[q:q + WIN - 6] = wide_ref[src, o + 3:o + WIN - 3]
                s4[q:q + WIN - 6] = wide_ref[src, a + 3:a + WIN - 3]
        in1_ref[src] = s1[...].astype(BF16)
        out1_ref[src] = s2[...].astype(BF16)
        out3_ref[src] = s3[...].astype(BF16)
        in3_ref[src] = s4[...].astype(BF16)
        return carry
    lax.fori_loop(0, GROUPS, one, 0)


def starts_of(lo, hi):
    out = list(range(lo, hi - 7, 8))
    if out[-1] + 8 < hi:
        out.append(hi - 8)
    return out


def relax_kernel(core_ref, owner_ref, f0, in1_ref, out3_ref, in3_ref, out1_ref, out_ref,
                 fi, fo3, fi3, fo, blk, den, t2s, t1s):
    cc = 1.0 / jacobi_diagonal
    d1, d2, d3 = jacobi_diagonal, jacobi_diagonal ** 2, jacobi_diagonal ** 3

    def widen(src):
        fi[...] = in1_ref[src].astype(F32)
        fo[...] = out1_ref[src].astype(F32)
        fo3[...] = out3_ref[src].astype(F32)
        fi3[...] = in3_ref[src].astype(F32)

    def span(z):
        return rows_of(max(H - z, z - H - 1, 0))

    def field(src, k, c, z, r):
        if z == 3 or z == 4:
            q = plane_row(z - 3, k, c) + r
            return f0[src, q:q + 8]
        if z == 2 or z == 5:
            q = near_row(k, c) + r - 1
            return (fo if z == 2 else fi)[q:q + 8]
        if z == 1 or z == 6:
            q = mid_row(k, c) + r - 2
            return (fo if z == 1 else fi)[q:q + 8]
        q = far_row(k, c) + r - 3
        return (fo3 if z == 0 else fi3)[q:q + 8]

    first = owner_ref[0]
    group = first // RES
    swap = (first % RES) == 1
    widen(group)
    for z in range(8):
        lo, hi = span(z)
        for r in starts_of(lo, hi):
            for c in range(COMPS):
                b0 = field(group, 0, c, z, r)
                b1 = field(group, 1, c, z, r)
                blk[0, z, c, r:r + 8] = jnp.where(swap, b1, b0)
                blk[1, z, c, r:r + 8] = jnp.where(swap, b0, b1)

    out_ref[...] = jnp.zeros(out_ref.shape, F32)
    core = core_ref[0]
    mids = starts_of(1, WIN - 1)

    def one_group(src, carry):
        widen(src)
        for k in range(RES):
            for z in range(8):
                lo, hi = span(z)
                for r in starts_of(lo, hi):
                    a = [field(src, k, c, z, r) for c in range(COMPS)]
                    for j in range(RES):
                        b = [blk[j, z, c, r:r + 8] for c in range(COMPS)]
                        den[2 * j, z, r:r + 8] = (a[0] * b[0] + a[1] * b[1]) + (a[2] * b[2] + a[3] * b[3])
                        den[2 * j + 1, z, r:r + 8] = (a[0] * b[1] - a[1] * b[0]) + (a[2] * b[3] - a[3] * b[2])

            def pair(q, z, d, r):
                return den[q, z - d, r:r + 8] + den[q, z + d, r:r + 8]

            def turned(t):
                return pltpu.roll(t, 1, 1) + pltpu.roll(t, LANES - 1, 1)

            scale = f0[src, BODY + 4 * k:BODY + 4 * k + 1] * (-0.25 * 0.25 * cc ** 4)
            scale = jnp.broadcast_to(scale, (8, LANES))
            for z in range(3, 5):
                t0 = {}
                for q in range(2 * RES):
                    kept = []
                    for r in mids:
                        e0 = den[q, z, r:r + 8]
                        e1 = pair(q, z, 1, r)
                        e2 = pair(q, z, 2, r)
                        plane = (den[q, z, r - 1:r + 7] + den[q, z, r + 1:r + 9]) + turned(e0)
                        t2 = (d1 * e0 + 3.0 * e1) + plane
                        t2s[q, z - 3, r:r + 8] = t2
                        kept.append((t2, ((d2 + 6.0) * e0 + (2.0 * d1) * e1) + 3.0 * e2))
                    for r, (t2, a1) in zip(mids, kept):
                        plane = (t2s[q, z - 3, r - 1:r + 7] + t2s[q, z - 3, r + 1:r + 9]) + turned(t2)
                        t1s[q, z - 3, r:r + 8] = a1 + plane
                    for r in starts_of(H, H + ROWS):
                        a0 = ((d3 + 2.0 * d1) * den[q, z, r:r + 8] + (d2 + 3.0) * pair(q, z, 1, r)) + (
                            d1 * pair(q, z, 2, r) + pair(q, z, 3, r))
                        plane = (t1s[q, z - 3, r - 1:r + 7] + t1s[q, z - 3, r + 1:r + 9]) + turned(t1s[q, z - 3, r:r + 8])
                        t0[q, r] = scale * (a0 + plane)
                p = core if z == 3 else 1 - core
                for r in starts_of(H, H + ROWS):
                    a = [field(src, k, c, z, r) for c in range(COMPS)]
                    for j in range(RES):
                        v = [t0[2 * j, r], t0[2 * j + 1, r]]
                        for s in range(2):
                            o = r - H
                            out_ref[j, 2 * s, p, o:o + 8] += a[2 * s] * v[0] - a[2 * s + 1] * v[1]
                            out_ref[j, 2 * s + 1, p, o:o + 8] += a[2 * s] * v[1] + a[2 * s + 1] * v[0]
        return carry
    lax.fori_loop(0, GROUPS, one_group, 0)


INTERPRET = False
KEEP = True
GRANT = 16 * 1024 * 1024


def on_device(bands, occ_level, block_owner):
    smem = pl.BlockSpec(memory_space=pltpu.SMEM)
    vmem = pl.BlockSpec(memory_space=pltpu.VMEM)

    def made(shape, dtype):
        return pltpu.VMEM(shape, dtype) if KEEP else jax.ShapeDtypeStruct(shape, dtype)

    def kept(value):
        return pltpu.with_memory_space_constraint(value, pltpu.VMEM) if KEEP else value

    x = bands.shape[3]
    place = lax.axis_index("space").astype(jnp.int32)
    core = (place & 1).reshape(1)
    send = pl.pallas_call(
        pack_kernel,
        out_shape=made((GROUPS, SEND, LANES), BF16),
        in_specs=[smem, vmem, smem], out_specs=vmem,
        scratch_shapes=[pltpu.VMEM((PLANES * RES * COMPS, x + 16, LANES), F32), pltpu.VMEM((SEND, LANES), F32)],
        interpret=INTERPRET, name="pack", compiler_params=pltpu.CompilerParams(vmem_limit_bytes=GRANT),
    )(core, bands.reshape(RES * COMPS * PLANES, x, LANES), occ_level)
    own = kept(lax.all_to_all(send, "band", 0, 0, tiled=True))

    sizes = (N1, N2, N2, N1)
    wide, in1, out3, in3, out1 = pl.pallas_call(
        cut_kernel,
        out_shape=[made((GROUPS, SEND, LANES), F32)] + [made((GROUPS, n, LANES), BF16) for n in sizes],
        in_specs=[vmem], out_specs=[vmem] * 5,
        scratch_shapes=[pltpu.VMEM((n, LANES), F32) for n in sizes],
        interpret=INTERPRET, name="cut", compiler_params=pltpu.CompilerParams(vmem_limit_bytes=GRANT),
    )(own)
    count = lax.axis_size("space")

    def shift(value, even, odd):
        return kept(lax.ppermute(value, "space", [(i, (i + (odd if i % 2 else even)) % count) for i in range(count)]))

    in1 = shift(in1, 1, -1)
    out3 = shift(out3, 2, -2)
    in3 = shift(in3, -2, 2)
    out1 = shift(out1, -1, 1)

    return pl.pallas_call(
        relax_kernel,
        out_shape=jax.ShapeDtypeStruct((RES, COMPS, PLANES, ROWS, LANES), F32),
        in_specs=[smem, smem] + [vmem] * 5, out_specs=vmem,
        scratch_shapes=[pltpu.VMEM((n, LANES), F32) for n in sizes] + [
            pltpu.VMEM((RES, 8, COMPS, 24, LANES), F32),
            pltpu.VMEM((2 * RES, 8, 24, LANES), F32),
            pltpu.VMEM((2 * RES, 2, 24, LANES), F32),
            pltpu.VMEM((2 * RES, 2, 24, LANES), F32)],
        interpret=INTERPRET, name="relax", compiler_params=pltpu.CompilerParams(vmem_limit_bytes=GRANT),
    )(core, block_owner, kept(wide), in1, out3, in3, out1)


def solution(mesh):
    return jax.shard_map(
        on_device,
        mesh=mesh,
        in_specs=(P("band", None, "space", None, None), P("band"), P()),
        out_specs=P(None, None, "space", "band", None),
        check_vma=False,
    )
```

```python
import jax
import jax.numpy as jnp
from jax import lax
from jax.experimental import pallas as pl
from jax.experimental.pallas import tpu as pltpu
from jax.sharding import PartitionSpec as P


SWEEPS = 4
jacobi_diagonal = 6.5

H = SWEEPS - 1
RES = 2
COMPS = 4
PLANES = 2
LANES = 128
GROUPS = 8
ROWS = 16
WIN = ROWS + 2 * H
BODY = PLANES * RES * COMPS * WIN
SEND = BODY + 8
F32 = jnp.float32
BF16 = jnp.bfloat16


def rows_of(d):
    return d, WIN - d


def plane_row(p, k, c):
    return ((p * RES + k) * COMPS + c) * WIN


N1 = RES * COMPS * ((WIN - 2) + (WIN - 4))
N2 = RES * COMPS * (WIN - 6)
NF = RES * 2 * RES * 2 * ROWS


def near_row(k, c):
    return (k * COMPS + c) * (WIN - 2)


def mid_row(k, c):
    return RES * COMPS * (WIN - 2) + (k * COMPS + c) * (WIN - 4)


def far_row(k, c):
    return (k * COMPS + c) * (WIN - 6)


def face_row(k, q, f):
    return ((k * 2 * RES + q) * 2 + f) * ROWS


OUTER, INNER, IN1, IN2, IN3 = range(5)
D1, D2, D3 = jacobi_diagonal, jacobi_diagonal ** 2, jacobi_diagonal ** 3


def pack_kernel(core_ref, bands_hbm, occ_hbm, out_ref, raw, occ_ref, ext, flat, sems, occ_sem):
    x = raw.shape[1]
    core = core_ref[0]
    levels = pltpu.make_async_copy(occ_hbm, occ_ref, occ_sem)
    levels.start()
    copies = [pltpu.make_async_copy(bands_hbm.at[pl.ds(PLANES * m, PLANES)], raw.at[pl.ds(PLANES * m, PLANES)], sems.at[m])
              for m in range(RES * COMPS)]
    for copy in copies:
        copy.start()
    for m, copy in enumerate(copies):
        copy.wait()
        for p in range(PLANES):
            plane = core if p == 0 else 1 - core
            n = p * RES * COMPS + m
            t = raw[m * PLANES + plane].astype(F32)
            ext[n, 8:8 + x] = t
            ext[n, 0:8] = t[x - 8:x]
            ext[n, 8 + x:16 + x] = t[0:8]
    levels.wait()
    for k in range(RES):
        flat[BODY + 4 * k:BODY + 4 * k + 4] = jnp.full((4, LANES), occ_ref[k].astype(F32), F32)
    for b in range(GROUPS):
        for n in range(PLANES * RES * COMPS):
            flat[n * WIN:(n + 1) * WIN] = ext[n, ROWS * b + 8 - H:ROWS * b + 8 - H + WIN]
        out_ref[b] = flat[...].astype(BF16)


def cut_kernel(own_ref, wide_ref, in1_ref, in3_ref, s1, s4):
    def one(src, carry):
        wide_ref[src] = own_ref[src].astype(F32)
        for k in range(RES):
            for c in range(COMPS):
                a = plane_row(0, k, c)
                o = plane_row(1, k, c)
                q = near_row(k, c)
                s1[q:q + WIN - 2] = wide_ref[src, o + 1:o + WIN - 1]
                q = mid_row(k, c)
                s1[q:q + WIN - 4] = wide_ref[src, a + 2:a + WIN - 2]
                q = far_row(k, c)
                s4[q:q + WIN - 6] = wide_ref[src, a + 3:a + WIN - 3]
        in1_ref[src] = s1[...].astype(BF16)
        in3_ref[src] = s4[...].astype(BF16)
        return carry

    lax.fori_loop(0, GROUPS, one, 0)


def starts_of(lo, hi):
    out = list(range(lo, hi - 7, 8))
    if out[-1] + 8 < hi:
        out.append(hi - 8)
    return out


def span(m):
    return rows_of(max(m - INNER, 0))


CORE_ROWS = starts_of(H, H + ROWS)


def field(f0, fi, fi3, src, k, c, m, r):
    if m in (OUTER, INNER):
        q = plane_row(m, k, c) + r
        return f0[src, q:q + 8]
    if m == IN1:
        q = near_row(k, c) + r - 1
        return fi[q:q + 8]
    if m == IN2:
        q = mid_row(k, c) + r - 2
        return fi[q:q + 8]
    q = far_row(k, c) + r - 3
    return fi3[q:q + 8]


def take_block(owner_ref, blk, planes, get):
    first = owner_ref[0]
    group = first // RES
    swap = (first % RES) == 1
    for i, m in enumerate(planes):
        for r in starts_of(*span(m)):
            for c in range(COMPS):
                b0 = get(group, 0, c, m, r)
                b1 = get(group, 1, c, m, r)
                blk[0, i, c, r:r + 8] = jnp.where(swap, b1, b0)
                blk[1, i, c, r:r + 8] = jnp.where(swap, b0, b1)


def densities(a, b):
    re = (a[0] * b[0] + a[1] * b[1]) + (a[2] * b[2] + a[3] * b[3])
    im = (a[0] * b[1] - a[1] * b[0]) + (a[2] * b[3] - a[3] * b[2])
    return re, im


def turned(t):
    return pltpu.roll(t, 1, 1) + pltpu.roll(t, LANES - 1, 1)


def face_kernel(owner_ref, f0, in1_ref, den, face_ref, fi, blk, lap, us):
    def get(src, k, c, m, r):
        return field(f0, fi, None, src, k, c, m, r)

    planes = (OUTER, INNER, IN1)
    fi[...] = in1_ref[owner_ref[0] // RES].astype(F32)
    take_block(owner_ref, blk, planes, get)

    def one_group(src, carry):
        fi[...] = in1_ref[src].astype(F32)
        for k in range(RES):
            i = src * RES + k
            for m in planes:
                for r in starts_of(*span(m)):
                    a = [get(src, k, c, m, r) for c in range(COMPS)]
                    for j in range(RES):
                        re, im = densities(a, [blk[j, m, c, r:r + 8] for c in range(COMPS)])
                        den[i, 2 * j, m, r:r + 8] = re
                        den[i, 2 * j + 1, m, r:r + 8] = im
            for q in range(2 * RES):
                for r in starts_of(2, WIN - 2):
                    e0 = den[i, q, OUTER, r:r + 8]
                    plane = (den[i, q, OUTER, r - 1:r + 7] + den[i, q, OUTER, r + 1:r + 9]) + turned(e0)
                    lap[k, q, r:r + 8] = plane
                    us[k, q, r:r + 8] = (2.0 * D1) * e0 + 3.0 * (den[i, q, INNER, r:r + 8] + plane)
                fa, fb = [], []
                for r in CORE_ROWS:
                    e0 = den[i, q, OUTER, r:r + 8]
                    e1 = den[i, q, INNER, r:r + 8]
                    plane = (us[k, q, r - 1:r + 7] + us[k, q, r + 1:r + 9]) + turned(us[k, q, r:r + 8])
                    fa.append(((D2 + 3.0) * e0 + D1 * e1) + (den[i, q, IN1, r:r + 8] + plane))
                    fb.append((D1 * e0 + e1) + 3.0 * lap[k, q, r:r + 8])
                for f, t in ((0, fa), (1, fb)):
                    o = face_row(k, q, f)
                    face_ref[src, o:o + ROWS] = jnp.concatenate(t, axis=0).astype(BF16)
        return carry

    lax.fori_loop(0, GROUPS, one_group, 0)


def scale_of(f0, src, k):
    level = f0[src, BODY + 4 * k:BODY + 4 * k + 1]
    return jnp.broadcast_to(level * (-0.25 * 0.25 / jacobi_diagonal ** 4), (8, LANES))


def add_products(out_ref, p, o, a, v):
    for j in range(RES):
        re, im = v[2 * j], v[2 * j + 1]
        for s in range(2):
            out_ref[j, 2 * s, p, o:o + 8] += a[2 * s] * re - a[2 * s + 1] * im
            out_ref[j, 2 * s + 1, p, o:o + 8] += a[2 * s] * im + a[2 * s + 1] * re


def local_kernel(owner_ref, f0, in1_ref, in3_ref, den, out_ref, fi, fi3, blk, d2s, t2s, t1s):
    def get(src, k, c, m, r):
        return field(f0, fi, fi3, src, k, c, m, r)

    def widen(src):
        fi[...] = in1_ref[src].astype(F32)
        fi3[...] = in3_ref[src].astype(F32)

    planes = (IN2, IN3)
    widen(owner_ref[0] // RES)
    take_block(owner_ref, blk, planes, get)
    out_ref[...] = jnp.zeros(out_ref.shape, F32)
    mids = starts_of(1, WIN - 1)

    def one_group(src, carry):
        widen(src)
        for k in range(RES):
            i = src * RES + k
            for z, m in enumerate(planes):
                for r in starts_of(*span(m)):
                    a = [get(src, k, c, m, r) for c in range(COMPS)]
                    for j in range(RES):
                        re, im = densities(a, [blk[j, z, c, r:r + 8] for c in range(COMPS)])
                        d2s[2 * j, z, r:r + 8] = re
                        d2s[2 * j + 1, z, r:r + 8] = im
            scale = scale_of(f0, src, k)

            def at(q, m, r):
                if m in planes:
                    return d2s[q, m - IN2, r:r + 8]
                return den[i, q, m, r:r + 8]

            def pair(q, z, d, r):
                t = at(q, z + d, r)
                return t + at(q, z - d, r) if z - d >= OUTER else t

            for z in (OUTER, INNER):
                t0 = {}
                for q in range(2 * RES):
                    kept = []
                    for r in mids:
                        e0 = at(q, z, r)
                        e1 = pair(q, z, 1, r)
                        e2 = pair(q, z, 2, r)
                        plane = (at(q, z, r - 1) + at(q, z, r + 1)) + turned(e0)
                        t2 = (D1 * e0 + 3.0 * e1) + plane
                        t2s[q, z, r:r + 8] = t2
                        kept.append((t2, ((D2 + 6.0) * e0 + (2.0 * D1) * e1) + 3.0 * e2))
                    for r, (t2, a1) in zip(mids, kept):
                        plane = (t2s[q, z, r - 1:r + 7] + t2s[q, z, r + 1:r + 9]) + turned(t2)
                        t1s[q, z, r:r + 8] = a1 + plane
                    for r in CORE_ROWS:
                        a0 = ((D3 + 2.0 * D1) * at(q, z, r) + (D2 + 3.0) * pair(q, z, 1, r)) + (
                            D1 * pair(q, z, 2, r) + at(q, z + 3, r))
                        plane = (t1s[q, z, r - 1:r + 7] + t1s[q, z, r + 1:r + 9]) + turned(t1s[q, z, r:r + 8])
                        t0[q, r] = scale * (a0 + plane)
                for r in CORE_ROWS:
                    a = [get(src, k, c, z, r) for c in range(COMPS)]
                    add_products(out_ref, z, r - H, a, [t0[q, r] for q in range(2 * RES)])
        return carry

    lax.fori_loop(0, GROUPS, one_group, 0)


def join_kernel(core_ref, f0, face_ref, part, out_ref, acc):
    acc[...] = part[...]

    def one_group(src, carry):
        for k in range(RES):
            scale = scale_of(f0, src, k)
            for z in (OUTER, INNER):
                got = []
                for q in range(2 * RES):
                    o = face_row(k, q, z)
                    got.append(face_ref[src, o:o + ROWS].astype(F32))
                for n, r in enumerate(CORE_ROWS):
                    a = [field(f0, None, None, src, k, c, z, r) * scale for c in range(COMPS)]
                    add_products(acc, z, r - H, a, [t[8 * n:8 * n + 8] for t in got])
        return carry

    lax.fori_loop(0, GROUPS, one_group, 0)
    core = core_ref[0]
    for j in range(RES):
        for c in range(COMPS):
            out_ref[j, c, core] = acc[j, c, OUTER]
            out_ref[j, c, 1 - core] = acc[j, c, INNER]


INTERPRET = False
KEEP = True
GRANT = 16 * 1024 * 1024


def on_device(bands, occ_level, block_owner):
    smem = pl.BlockSpec(memory_space=pltpu.SMEM)
    vmem = pl.BlockSpec(memory_space=pltpu.VMEM)
    hbm = pl.BlockSpec(memory_space=pltpu.HBM if KEEP else pl.ANY)

    def made(shape, dtype):
        return pltpu.VMEM(shape, dtype) if KEEP else jax.ShapeDtypeStruct(shape, dtype)

    def kept(value):
        return pltpu.with_memory_space_constraint(value, pltpu.VMEM) if KEEP else value

    def in_hbm(value):
        return pltpu.with_memory_space_constraint(value, pltpu.HBM) if KEEP else value

    def call(kernel, out_shape, in_specs, scratch):
        out_specs = [vmem] * len(out_shape) if isinstance(out_shape, list) else vmem
        return pl.pallas_call(
            kernel, out_shape=out_shape, in_specs=in_specs, out_specs=out_specs,
            scratch_shapes=scratch, interpret=INTERPRET,
            compiler_params=pltpu.CompilerParams(vmem_limit_bytes=GRANT))

    x = bands.shape[3]
    place = lax.axis_index("space").astype(jnp.int32)
    core = (place & 1).reshape(1)
    send = call(
        pack_kernel, made((GROUPS, SEND, LANES), BF16), [smem, hbm, hbm],
        [pltpu.VMEM((RES * COMPS * PLANES, x, LANES), BF16), pltpu.SMEM((RES,), jnp.int32),
         pltpu.VMEM((PLANES * RES * COMPS, x + 16, LANES), F32), pltpu.VMEM((SEND, LANES), F32),
         pltpu.SemaphoreType.DMA((RES * COMPS,)), pltpu.SemaphoreType.DMA],
    )(core, in_hbm(bands.reshape(RES * COMPS * PLANES, x, LANES)), in_hbm(occ_level))
    own = kept(lax.all_to_all(send, "band", 0, 0, tiled=True))

    wide, in1, in3 = call(
        cut_kernel,
        [made((GROUPS, SEND, LANES), F32), made((GROUPS, N1, LANES), BF16), made((GROUPS, N2, LANES), BF16)],
        [vmem], [pltpu.VMEM((N1, LANES), F32), pltpu.VMEM((N2, LANES), F32)],
    )(own)
    wide = kept(wide)
    count = lax.axis_size("space")

    def shift(value, even, odd):
        pairs = [(i, (i + (odd if i % 2 else even)) % count) for i in range(count)]
        value = lax.ppermute(value, "space", pairs)
        return kept(value)

    in1 = shift(in1, 1, -1)
    in3 = shift(in3, -2, 2)

    den, face = call(
        face_kernel,
        [made((GROUPS * RES, 2 * RES, 3, 24, LANES), F32), made((GROUPS, NF, LANES), BF16)],
        [smem] + [vmem] * 2,
        [pltpu.VMEM((N1, LANES), F32), pltpu.VMEM((RES, 3, COMPS, 24, LANES), F32),
         pltpu.VMEM((RES, 2 * RES, 24, LANES), F32), pltpu.VMEM((RES, 2 * RES, 24, LANES), F32)],
    )(block_owner, wide, in1)
    face = shift(face, -1, 1)

    part = call(
        local_kernel, made((RES, COMPS, PLANES, ROWS, LANES), F32),
        [smem] + [vmem] * 4,
        [pltpu.VMEM((N1, LANES), F32), pltpu.VMEM((N2, LANES), F32),
         pltpu.VMEM((RES, 2, COMPS, 24, LANES), F32)] + [pltpu.VMEM((2 * RES, 2, 24, LANES), F32)] * 3,
    )(block_owner, wide, in1, in3, kept(den))

    return call(
        join_kernel, jax.ShapeDtypeStruct((RES, COMPS, PLANES, ROWS, LANES), F32),
        [smem] + [vmem] * 3, [pltpu.VMEM((RES, COMPS, PLANES, ROWS, LANES), F32)],
    )(core, wide, face, kept(part))


def solution(mesh):
    return jax.shard_map(
        on_device,
        mesh=mesh,
        in_specs=(P("band", None, "space", None, None), P("band"), P()),
        out_specs=P(None, None, "space", "band", None),
        check_vma=False,
    )
```

```python
import jax
import jax.numpy as jnp
from jax import lax
from jax.experimental import pallas as pl
from jax.experimental.pallas import tpu as pltpu
from jax.sharding import PartitionSpec as P


SWEEPS = 4
jacobi_diagonal = 6.5

H = SWEEPS - 1
RES = 2
COMPS = 4
PLANES = 2
LANES = 128
GROUPS = 8
ROWS = 16
WIN = ROWS + 2 * H
BODY = PLANES * RES * COMPS * WIN
SEND = BODY + 8
F32 = jnp.float32
BF16 = jnp.bfloat16


def rows_of(d):
    return d, WIN - d


def plane_row(p, k, c):
    return ((p * RES + k) * COMPS + c) * WIN


N1 = RES * COMPS * ((WIN - 2) + (WIN - 4))
N2 = RES * COMPS * (WIN - 6)
NF = RES * 2 * RES * 2 * ROWS


def near_row(k, c):
    return (k * COMPS + c) * (WIN - 2)


def mid_row(k, c):
    return RES * COMPS * (WIN - 2) + (k * COMPS + c) * (WIN - 4)


def far_row(k, c):
    return (k * COMPS + c) * (WIN - 6)


def face_row(k, q, f):
    return ((k * 2 * RES + q) * 2 + f) * ROWS


OUTER, INNER, IN1, IN2, IN3 = range(5)
D1, D2, D3 = jacobi_diagonal, jacobi_diagonal ** 2, jacobi_diagonal ** 3


def pack_kernel(core_ref, bands_hbm, occ_hbm, out_ref, raw, occ_ref, ext, flat, sems, occ_sem):
    x = raw.shape[1]
    core = core_ref[0]
    levels = pltpu.make_async_copy(occ_hbm, occ_ref, occ_sem)
    levels.start()
    copies = [pltpu.make_async_copy(bands_hbm.at[pl.ds(PLANES * m, PLANES)], raw.at[pl.ds(PLANES * m, PLANES)], sems.at[m])
              for m in range(RES * COMPS)]
    for copy in copies:
        copy.start()
    for m, copy in enumerate(copies):
        copy.wait()
        for p in range(PLANES):
            plane = core if p == 0 else 1 - core
            n = p * RES * COMPS + m
            t = raw[m * PLANES + plane].astype(F32)
            ext[n, 8:8 + x] = t
            ext[n, 0:8] = t[x - 8:x]
            ext[n, 8 + x:16 + x] = t[0:8]
    levels.wait()
    for k in range(RES):
        flat[BODY + 4 * k:BODY + 4 * k + 4] = jnp.full((4, LANES), occ_ref[k].astype(F32), F32)
    for b in range(GROUPS):
        for n in range(PLANES * RES * COMPS):
            flat[n * WIN:(n + 1) * WIN] = ext[n, ROWS * b + 8 - H:ROWS * b + 8 - H + WIN]
        out_ref[b] = flat[...].astype(BF16)


def cut_kernel(own_ref, wide_ref, in1_ref, in3_ref, s1, s4):
    def one(src, carry):
        wide_ref[src] = own_ref[src].astype(F32)
        for k in range(RES):
            for c in range(COMPS):
                a = plane_row(0, k, c)
                o = plane_row(1, k, c)
                q = near_row(k, c)
                s1[q:q + WIN - 2] = wide_ref[src, o + 1:o + WIN - 1]
                q = mid_row(k, c)
                s1[q:q + WIN - 4] = wide_ref[src, a + 2:a + WIN - 2]
                q = far_row(k, c)
                s4[q:q + WIN - 6] = wide_ref[src, a + 3:a + WIN - 3]
        in1_ref[src] = s1[...].astype(BF16)
        in3_ref[src] = s4[...].astype(BF16)
        return carry

    lax.fori_loop(0, GROUPS, one, 0)


def starts_of(lo, hi):
    out = list(range(lo, hi - 7, 8))
    if out[-1] + 8 < hi:
        out.append(hi - 8)
    return out


def span(m):
    return rows_of(max(m - INNER, 0))


CORE_ROWS = starts_of(H, H + ROWS)


def field(f0, fi, fi3, src, k, c, m, r):
    if m in (OUTER, INNER):
        q = plane_row(m, k, c) + r
        return f0[src, q:q + 8]
    if m == IN1:
        q = near_row(k, c) + r - 1
        return fi[q:q + 8]
    if m == IN2:
        q = mid_row(k, c) + r - 2
        return fi[q:q + 8]
    q = far_row(k, c) + r - 3
    return fi3[q:q + 8]


def take_block(owner_ref, blk, planes, get):
    first = owner_ref[0]
    group = first // RES
    swap = (first % RES) == 1
    for i, m in enumerate(planes):
        for r in starts_of(*span(m)):
            for c in range(COMPS):
                b0 = get(group, 0, c, m, r)
                b1 = get(group, 1, c, m, r)
                blk[0, i, c, r:r + 8] = jnp.where(swap, b1, b0)
                blk[1, i, c, r:r + 8] = jnp.where(swap, b0, b1)


def densities(a, b):
    re = (a[0] * b[0] + a[1] * b[1]) + (a[2] * b[2] + a[3] * b[3])
    im = (a[0] * b[1] - a[1] * b[0]) + (a[2] * b[3] - a[3] * b[2])
    return re, im


def turned(t):
    return pltpu.roll(t, 1, 1) + pltpu.roll(t, LANES - 1, 1)


def own_face_kernel(owner_ref, f0, den, fab, blk, lap, us):
    def get(src, k, c, m, r):
        return field(f0, None, None, src, k, c, m, r)

    planes = (OUTER, INNER)
    take_block(owner_ref, blk, planes, get)

    def one_group(src, carry):
        for k in range(RES):
            i = src * RES + k
            for m in planes:
                for r in starts_of(*span(m)):
                    a = [get(src, k, c, m, r) for c in range(COMPS)]
                    for j in range(RES):
                        re, im = densities(a, [blk[j, m, c, r:r + 8] for c in range(COMPS)])
                        den[i, 2 * j, m, r:r + 8] = re
                        den[i, 2 * j + 1, m, r:r + 8] = im
            for q in range(2 * RES):
                for r in starts_of(2, WIN - 2):
                    e0 = den[i, q, OUTER, r:r + 8]
                    plane = (den[i, q, OUTER, r - 1:r + 7] + den[i, q, OUTER, r + 1:r + 9]) + turned(e0)
                    lap[k, q, r:r + 8] = plane
                    us[k, q, r:r + 8] = (2.0 * D1) * e0 + 3.0 * (den[i, q, INNER, r:r + 8] + plane)
                for n, r in enumerate(CORE_ROWS):
                    e0 = den[i, q, OUTER, r:r + 8]
                    e1 = den[i, q, INNER, r:r + 8]
                    plane = (us[k, q, r - 1:r + 7] + us[k, q, r + 1:r + 9]) + turned(us[k, q, r:r + 8])
                    o = face_row(k, q, 0) + 8 * n
                    fab[src, o:o + 8] = ((D2 + 3.0) * e0 + D1 * e1) + plane
                    o = face_row(k, q, 1) + 8 * n
                    fab[src, o:o + 8] = (D1 * e0 + e1) + 3.0 * lap[k, q, r:r + 8]
        return carry

    lax.fori_loop(0, GROUPS, one_group, 0)


def face_kernel(owner_ref, fab, in1_ref, den1, face_ref, fi, blk):
    def get(src, k, c, m, r):
        return field(None, fi, None, src, k, c, m, r)

    fi[...] = in1_ref[owner_ref[0] // RES].astype(F32)
    take_block(owner_ref, blk, (IN1,), get)

    def one_group(src, carry):
        near = RES * COMPS * (WIN - 2)
        fi[0:near] = in1_ref[src, 0:near].astype(F32)
        for k in range(RES):
            i = src * RES + k
            for r in starts_of(*span(IN1)):
                a = [get(src, k, c, IN1, r) for c in range(COMPS)]
                for j in range(RES):
                    re, im = densities(a, [blk[j, 0, c, r:r + 8] for c in range(COMPS)])
                    den1[i, 2 * j, r:r + 8] = re
                    den1[i, 2 * j + 1, r:r + 8] = im
            for q in range(2 * RES):
                o = face_row(k, q, 0)
                face_ref[src, o:o + ROWS] = (fab[src, o:o + ROWS] + den1[i, q, H:H + ROWS]).astype(BF16)
                o = face_row(k, q, 1)
                face_ref[src, o:o + ROWS] = fab[src, o:o + ROWS].astype(BF16)
        return carry

    lax.fori_loop(0, GROUPS, one_group, 0)


def scale_of(f0, src, k):
    level = f0[src, BODY + 4 * k:BODY + 4 * k + 1]
    return jnp.broadcast_to(level * (-0.25 * 0.25 / jacobi_diagonal ** 4), (8, LANES))


def add_products(out_ref, p, o, a, v):
    for j in range(RES):
        re, im = v[2 * j], v[2 * j + 1]
        for s in range(2):
            out_ref[j, 2 * s, p, o:o + 8] += a[2 * s] * re - a[2 * s + 1] * im
            out_ref[j, 2 * s + 1, p, o:o + 8] += a[2 * s] * im + a[2 * s + 1] * re


def local_kernel(owner_ref, f0, in1_ref, den, den1, out_ref, fi, blk, d2s, t2s, t1s):
    def get(src, k, c, m, r):
        return field(f0, fi, None, src, k, c, m, r)

    def widen(src):
        fi[...] = in1_ref[src].astype(F32)

    planes = (IN2,)
    widen(owner_ref[0] // RES)
    take_block(owner_ref, blk, planes, get)
    out_ref[...] = jnp.zeros(out_ref.shape, F32)
    mids = starts_of(1, WIN - 1)

    def one_group(src, carry):
        widen(src)
        for k in range(RES):
            i = src * RES + k
            for z, m in enumerate(planes):
                for r in starts_of(*span(m)):
                    a = [get(src, k, c, m, r) for c in range(COMPS)]
                    for j in range(RES):
                        re, im = densities(a, [blk[j, z, c, r:r + 8] for c in range(COMPS)])
                        d2s[2 * j, z, r:r + 8] = re
                        d2s[2 * j + 1, z, r:r + 8] = im
            scale = scale_of(f0, src, k)

            def at(q, m, r):
                if m == IN2:
                    return d2s[q, 0, r:r + 8]
                if m == IN1:
                    return den1[i, q, r:r + 8]
                return den[i, q, m, r:r + 8]

            def pair(q, z, d, r):
                t = at(q, z + d, r)
                return t + at(q, z - d, r) if z - d >= OUTER else t

            for z in (OUTER, INNER):
                t0 = {}
                for q in range(2 * RES):
                    kept = []
                    for r in mids:
                        e0 = at(q, z, r)
                        e1 = pair(q, z, 1, r)
                        e2 = pair(q, z, 2, r)
                        plane = (at(q, z, r - 1) + at(q, z, r + 1)) + turned(e0)
                        t2 = (D1 * e0 + 3.0 * e1) + plane
                        t2s[q, z, r:r + 8] = t2
                        kept.append((t2, ((D2 + 6.0) * e0 + (2.0 * D1) * e1) + 3.0 * e2))
                    for r, (t2, a1) in zip(mids, kept):
                        plane = (t2s[q, z, r - 1:r + 7] + t2s[q, z, r + 1:r + 9]) + turned(t2)
                        t1s[q, z, r:r + 8] = a1 + plane
                    for r in CORE_ROWS:
                        a0 = ((D3 + 2.0 * D1) * at(q, z, r) + (D2 + 3.0) * pair(q, z, 1, r)) + D1 * pair(q, z, 2, r)
                        if z + 3 <= IN2:
                            a0 = a0 + at(q, z + 3, r)
                        plane = (t1s[q, z, r - 1:r + 7] + t1s[q, z, r + 1:r + 9]) + turned(t1s[q, z, r:r + 8])
                        t0[q, r] = scale * (a0 + plane)
                for r in CORE_ROWS:
                    a = [get(src, k, c, z, r) for c in range(COMPS)]
                    add_products(out_ref, z, r - H, a, [t0[q, r] for q in range(2 * RES)])
        return carry

    lax.fori_loop(0, GROUPS, one_group, 0)


def join_kernel(core_ref, owner_ref, f0, in3_ref, face_ref, part, out_ref, acc, fi3, blk):
    def get(src, k, c, m, r):
        return field(f0, None, fi3, src, k, c, m, r)

    fi3[...] = in3_ref[owner_ref[0] // RES].astype(F32)
    take_block(owner_ref, blk, (IN3,), get)
    acc[...] = part[...]

    def one_group(src, carry):
        fi3[...] = in3_ref[src].astype(F32)
        for k in range(RES):
            scale = scale_of(f0, src, k)
            for z in (OUTER, INNER):
                got = []
                for q in range(2 * RES):
                    o = face_row(k, q, z)
                    got.append(face_ref[src, o:o + ROWS].astype(F32))
                for n, r in enumerate(CORE_ROWS):
                    v = [t[8 * n:8 * n + 8] for t in got]
                    if z == INNER:
                        far = [get(src, k, c, IN3, r) for c in range(COMPS)]
                        for j in range(RES):
                            re, im = densities(far, [blk[j, 0, c, r:r + 8] for c in range(COMPS)])
                            v[2 * j] = v[2 * j] + re
                            v[2 * j + 1] = v[2 * j + 1] + im
                    a = [get(src, k, c, z, r) * scale for c in range(COMPS)]
                    add_products(acc, z, r - H, a, v)
        return carry

    lax.fori_loop(0, GROUPS, one_group, 0)
    core = core_ref[0]
    for j in range(RES):
        for c in range(COMPS):
            out_ref[j, c, core] = acc[j, c, OUTER]
            out_ref[j, c, 1 - core] = acc[j, c, INNER]


INTERPRET = False
KEEP = True
GRANT = 16 * 1024 * 1024


def on_device(bands, occ_level, block_owner):
    smem = pl.BlockSpec(memory_space=pltpu.SMEM)
    vmem = pl.BlockSpec(memory_space=pltpu.VMEM)
    hbm = pl.BlockSpec(memory_space=pltpu.HBM if KEEP else pl.ANY)

    def made(shape, dtype):
        return pltpu.VMEM(shape, dtype) if KEEP else jax.ShapeDtypeStruct(shape, dtype)

    def kept(value):
        return pltpu.with_memory_space_constraint(value, pltpu.VMEM) if KEEP else value

    def in_hbm(value):
        return pltpu.with_memory_space_constraint(value, pltpu.HBM) if KEEP else value

    def call(kernel, out_shape, in_specs, scratch):
        out_specs = [vmem] * len(out_shape) if isinstance(out_shape, list) else vmem
        return pl.pallas_call(
            kernel, out_shape=out_shape, in_specs=in_specs, out_specs=out_specs,
            scratch_shapes=scratch, interpret=INTERPRET,
            compiler_params=pltpu.CompilerParams(vmem_limit_bytes=GRANT))

    x = bands.shape[3]
    place = lax.axis_index("space").astype(jnp.int32)
    core = (place & 1).reshape(1)
    send = call(
        pack_kernel, made((GROUPS, SEND, LANES), BF16), [smem, hbm, hbm],
        [pltpu.VMEM((RES * COMPS * PLANES, x, LANES), BF16), pltpu.SMEM((RES,), jnp.int32),
         pltpu.VMEM((PLANES * RES * COMPS, x + 16, LANES), F32), pltpu.VMEM((SEND, LANES), F32),
         pltpu.SemaphoreType.DMA((RES * COMPS,)), pltpu.SemaphoreType.DMA],
    )(core, in_hbm(bands.reshape(RES * COMPS * PLANES, x, LANES)), in_hbm(occ_level))
    own = kept(lax.all_to_all(send, "band", 0, 0, tiled=True))

    wide, in1, in3 = call(
        cut_kernel,
        [made((GROUPS, SEND, LANES), F32), made((GROUPS, N1, LANES), BF16), made((GROUPS, N2, LANES), BF16)],
        [vmem], [pltpu.VMEM((N1, LANES), F32), pltpu.VMEM((N2, LANES), F32)],
    )(own)
    wide = kept(wide)
    count = lax.axis_size("space")

    def shift(value, even, odd):
        pairs = [(i, (i + (odd if i % 2 else even)) % count) for i in range(count)]
        value = lax.ppermute(value, "space", pairs)
        return kept(value)

    in1 = shift(in1, 1, -1)

    den, fab = call(
        own_face_kernel,
        [made((GROUPS * RES, 2 * RES, 2, 24, LANES), F32), made((GROUPS, NF, LANES), F32)],
        [smem, vmem],
        [pltpu.VMEM((RES, 2, COMPS, 24, LANES), F32), pltpu.VMEM((RES, 2 * RES, 24, LANES), F32),
         pltpu.VMEM((RES, 2 * RES, 24, LANES), F32)],
    )(block_owner, wide)
    den1, face = call(
        face_kernel,
        [made((GROUPS * RES, 2 * RES, 24, LANES), F32), made((GROUPS, NF, LANES), BF16)],
        [smem] + [vmem] * 2,
        [pltpu.VMEM((N1, LANES), F32), pltpu.VMEM((RES, 1, COMPS, 24, LANES), F32)],
    )(block_owner, kept(fab), in1)
    face = shift(face, -1, 1)

    part = call(
        local_kernel, made((RES, COMPS, PLANES, ROWS, LANES), F32),
        [smem] + [vmem] * 4,
        [pltpu.VMEM((N1, LANES), F32), pltpu.VMEM((RES, 1, COMPS, 24, LANES), F32),
         pltpu.VMEM((2 * RES, 1, 24, LANES), F32)] + [pltpu.VMEM((2 * RES, 2, 24, LANES), F32)] * 2,
    )(block_owner, wide, in1, kept(den), kept(den1))
    in3 = shift(in3, -2, 2)

    return call(
        join_kernel, jax.ShapeDtypeStruct((RES, COMPS, PLANES, ROWS, LANES), F32),
        [smem, smem] + [vmem] * 4,
        [pltpu.VMEM((RES, COMPS, PLANES, ROWS, LANES), F32), pltpu.VMEM((N2, LANES), F32),
         pltpu.VMEM((RES, 1, COMPS, 24, LANES), F32)],
    )(core, block_owner, wide, in3, face, kept(part))


def solution(mesh):
    return jax.shard_map(
        on_device,
        mesh=mesh,
        in_specs=(P("band", None, "space", None, None), P("band"), P()),
        out_specs=P(None, None, "space", "band", None),
        check_vma=False,
    )
```

```python
import jax
import jax.numpy as jnp
from jax import lax
from jax.experimental import pallas as pl
from jax.experimental.pallas import tpu as pltpu
from jax.sharding import PartitionSpec as P


SWEEPS = 4
jacobi_diagonal = 6.5

H = SWEEPS - 1
RES = 2
COMPS = 4
PLANES = 2
LANES = 128
GROUPS = 8
ROWS = 16
WIN = ROWS + 2 * H
BODY = PLANES * RES * COMPS * WIN
SEND = BODY + 8
F32 = jnp.float32
BF16 = jnp.bfloat16


def rows_of(d):
    return d, WIN - d


def plane_row(p, k, c):
    return ((p * RES + k) * COMPS + c) * WIN


N1 = RES * COMPS * ((WIN - 2) + (WIN - 4))
N2 = RES * COMPS * (WIN - 6)
NF = RES * 2 * RES * 2 * ROWS


def near_row(k, c):
    return (k * COMPS + c) * (WIN - 2)


def mid_row(k, c):
    return RES * COMPS * (WIN - 2) + (k * COMPS + c) * (WIN - 4)


def far_row(k, c):
    return (k * COMPS + c) * (WIN - 6)


def face_row(k, q, f):
    return ((k * 2 * RES + q) * 2 + f) * ROWS


OUTER, INNER, IN1, IN2, IN3 = range(5)
D1, D2, D3 = jacobi_diagonal, jacobi_diagonal ** 2, jacobi_diagonal ** 3


def pack_kernel(core_ref, bands_hbm, occ_hbm, out_ref, raw, occ_ref, ext, flat, sems, occ_sem):
    x = raw.shape[1]
    core = core_ref[0]
    levels = pltpu.make_async_copy(occ_hbm, occ_ref, occ_sem)
    levels.start()
    copies = [pltpu.make_async_copy(bands_hbm.at[pl.ds(PLANES * m, PLANES)], raw.at[pl.ds(PLANES * m, PLANES)], sems.at[m])
              for m in range(RES * COMPS)]
    for copy in copies:
        copy.start()
    for m, copy in enumerate(copies):
        copy.wait()
        for p in range(PLANES):
            plane = core if p == 0 else 1 - core
            n = p * RES * COMPS + m
            t = raw[m * PLANES + plane].astype(F32)
            ext[n, 8:8 + x] = t
            ext[n, 0:8] = t[x - 8:x]
            ext[n, 8 + x:16 + x] = t[0:8]
    levels.wait()
    for k in range(RES):
        flat[BODY + 4 * k:BODY + 4 * k + 4] = jnp.full((4, LANES), occ_ref[k].astype(F32), F32)
    for b in range(GROUPS):
        for n in range(PLANES * RES * COMPS):
            flat[n * WIN:(n + 1) * WIN] = ext[n, ROWS * b + 8 - H:ROWS * b + 8 - H + WIN]
        out_ref[b] = flat[...].astype(BF16)


def cut_kernel(own_ref, wide_ref, in1_ref, in3_ref, s1, s4):
    def one(src, carry):
        wide_ref[src] = own_ref[src].astype(F32)
        for k in range(RES):
            for c in range(COMPS):
                a = plane_row(0, k, c)
                o = plane_row(1, k, c)
                q = near_row(k, c)
                s1[q:q + WIN - 2] = wide_ref[src, o + 1:o + WIN - 1]
                q = mid_row(k, c)
                s1[q:q + WIN - 4] = wide_ref[src, a + 2:a + WIN - 2]
                q = far_row(k, c)
                s4[q:q + WIN - 6] = wide_ref[src, a + 3:a + WIN - 3]
        in1_ref[src] = s1[...].astype(BF16)
        in3_ref[src] = s4[...].astype(BF16)
        return carry

    lax.fori_loop(0, GROUPS, one, 0)


def starts_of(lo, hi):
    out = list(range(lo, hi - 7, 8))
    if out[-1] + 8 < hi:
        out.append(hi - 8)
    return out


def span(m):
    return rows_of(max(m - INNER, 0))


CORE_ROWS = starts_of(H, H + ROWS)


def field(f0, fi, fi3, src, k, c, m, r):
    if m in (OUTER, INNER):
        q = plane_row(m, k, c) + r
        return f0[src, q:q + 8]
    if m == IN1:
        q = near_row(k, c) + r - 1
        return fi[q:q + 8]
    if m == IN2:
        q = mid_row(k, c) + r - 2
        return fi[q:q + 8]
    q = far_row(k, c) + r - 3
    return fi3[q:q + 8]


def take_block(owner_ref, blk, planes, get):
    first = owner_ref[0]
    group = first // RES
    swap = (first % RES) == 1
    for i, m in enumerate(planes):
        for r in starts_of(*span(m)):
            for c in range(COMPS):
                b0 = get(group, 0, c, m, r)
                b1 = get(group, 1, c, m, r)
                blk[0, i, c, r:r + 8] = jnp.where(swap, b1, b0)
                blk[1, i, c, r:r + 8] = jnp.where(swap, b0, b1)


def densities(a, b):
    re = (a[0] * b[0] + a[1] * b[1]) + (a[2] * b[2] + a[3] * b[3])
    im = (a[0] * b[1] - a[1] * b[0]) + (a[2] * b[3] - a[3] * b[2])
    return re, im


def turned(t):
    return pltpu.roll(t, 1, 1) + pltpu.roll(t, LANES - 1, 1)


def own_face_kernel(owner_ref, f0, den, fab, blk, lap, us):
    def get(src, k, c, m, r):
        return field(f0, None, None, src, k, c, m, r)

    planes = (OUTER, INNER)
    take_block(owner_ref, blk, planes, get)

    def one_group(src, carry):
        for k in range(RES):
            i = src * RES + k
            for m in planes:
                for r in starts_of(*span(m)):
                    a = [get(src, k, c, m, r) for c in range(COMPS)]
                    for j in range(RES):
                        re, im = densities(a, [blk[j, m, c, r:r + 8] for c in range(COMPS)])
                        den[i, 2 * j, m, r:r + 8] = re
                        den[i, 2 * j + 1, m, r:r + 8] = im
            for q in range(2 * RES):
                for r in starts_of(2, WIN - 2):
                    e0 = den[i, q, OUTER, r:r + 8]
                    plane = (den[i, q, OUTER, r - 1:r + 7] + den[i, q, OUTER, r + 1:r + 9]) + turned(e0)
                    lap[k, q, r:r + 8] = plane
                    us[k, q, r:r + 8] = (2.0 * D1) * e0 + 3.0 * (den[i, q, INNER, r:r + 8] + plane)
                for n, r in enumerate(CORE_ROWS):
                    e0 = den[i, q, OUTER, r:r + 8]
                    e1 = den[i, q, INNER, r:r + 8]
                    plane = (us[k, q, r - 1:r + 7] + us[k, q, r + 1:r + 9]) + turned(us[k, q, r:r + 8])
                    o = face_row(k, q, 0) + 8 * n
                    fab[src, o:o + 8] = ((D2 + 3.0) * e0 + D1 * e1) + plane
                    o = face_row(k, q, 1) + 8 * n
                    fab[src, o:o + 8] = (D1 * e0 + e1) + 3.0 * lap[k, q, r:r + 8]
        return carry

    lax.fori_loop(0, GROUPS, one_group, 0)


def face_kernel(owner_ref, fab, in1_ref, den1, face_ref, fi, blk):
    def get(src, k, c, m, r):
        return field(None, fi, None, src, k, c, m, r)

    fi[...] = in1_ref[owner_ref[0] // RES].astype(F32)
    take_block(owner_ref, blk, (IN1,), get)

    def one_group(src, carry):
        near = RES * COMPS * (WIN - 2)
        fi[0:near] = in1_ref[src, 0:near].astype(F32)
        for k in range(RES):
            i = src * RES + k
            for r in starts_of(*span(IN1)):
                a = [get(src, k, c, IN1, r) for c in range(COMPS)]
                for j in range(RES):
                    re, im = densities(a, [blk[j, 0, c, r:r + 8] for c in range(COMPS)])
                    den1[i, 2 * j, r:r + 8] = re
                    den1[i, 2 * j + 1, r:r + 8] = im
            for q in range(2 * RES):
                o = face_row(k, q, 0)
                face_ref[src, o:o + ROWS] = (fab[src, o:o + ROWS] + den1[i, q, H:H + ROWS]).astype(BF16)
                o = face_row(k, q, 1)
                face_ref[src, o:o + ROWS] = fab[src, o:o + ROWS].astype(BF16)
        return carry

    lax.fori_loop(0, GROUPS, one_group, 0)


def scale_of(f0, src, k):
    level = f0[src, BODY + 4 * k:BODY + 4 * k + 1]
    return jnp.broadcast_to(level * (-0.25 * 0.25 / jacobi_diagonal ** 4), (8, LANES))


def add_products(out_ref, p, o, a, v):
    for j in range(RES):
        re, im = v[2 * j], v[2 * j + 1]
        for s in range(2):
            out_ref[j, 2 * s, p, o:o + 8] += a[2 * s] * re - a[2 * s + 1] * im
            out_ref[j, 2 * s + 1, p, o:o + 8] += a[2 * s] * im + a[2 * s + 1] * re


def local_kernel(owner_ref, f0, in1_ref, den, den1, out_ref, fi, blk, d2s, t2s, t1s):
    def get(src, k, c, m, r):
        return field(f0, fi, None, src, k, c, m, r)

    def widen(src):
        fi[...] = in1_ref[src].astype(F32)

    planes = (IN2,)
    widen(owner_ref[0] // RES)
    take_block(owner_ref, blk, planes, get)
    out_ref[...] = jnp.zeros(out_ref.shape, F32)
    mids = starts_of(1, WIN - 1)

    def one_group(src, carry):
        widen(src)
        for k in range(RES):
            i = src * RES + k
            for z, m in enumerate(planes):
                for r in starts_of(*span(m)):
                    a = [get(src, k, c, m, r) for c in range(COMPS)]
                    for j in range(RES):
                        re, im = densities(a, [blk[j, z, c, r:r + 8] for c in range(COMPS)])
                        d2s[2 * j, z, r:r + 8] = re
                        d2s[2 * j + 1, z, r:r + 8] = im
            scale = scale_of(f0, src, k)

            def at(q, m, r):
                if m == IN2:
                    return d2s[q, 0, r:r + 8]
                if m == IN1:
                    return den1[i, q, r:r + 8]
                return den[i, q, m, r:r + 8]

            def pair(q, z, d, r):
                t = at(q, z + d, r)
                return t + at(q, z - d, r) if z - d >= OUTER else t

            for z in (OUTER, INNER):
                t0 = {}
                for q in range(2 * RES):
                    kept = []
                    for r in mids:
                        e0 = at(q, z, r)
                        e1 = pair(q, z, 1, r)
                        e2 = pair(q, z, 2, r)
                        plane = (at(q, z, r - 1) + at(q, z, r + 1)) + turned(e0)
                        t2 = (D1 * e0 + 3.0 * e1) + plane
                        t2s[q, z, r:r + 8] = t2
                        kept.append((t2, ((D2 + 6.0) * e0 + (2.0 * D1) * e1) + 3.0 * e2))
                    for r, (t2, a1) in zip(mids, kept):
                        plane = (t2s[q, z, r - 1:r + 7] + t2s[q, z, r + 1:r + 9]) + turned(t2)
                        t1s[q, z, r:r + 8] = a1 + plane
                    for r in CORE_ROWS:
                        a0 = ((D3 + 2.0 * D1) * at(q, z, r) + (D2 + 3.0) * pair(q, z, 1, r)) + D1 * pair(q, z, 2, r)
                        if z + 3 <= IN2:
                            a0 = a0 + at(q, z + 3, r)
                        plane = (t1s[q, z, r - 1:r + 7] + t1s[q, z, r + 1:r + 9]) + turned(t1s[q, z, r:r + 8])
                        t0[q, r] = scale * (a0 + plane)
                for r in CORE_ROWS:
                    a = [get(src, k, c, z, r) for c in range(COMPS)]
                    add_products(out_ref, z, r - H, a, [t0[q, r] for q in range(2 * RES)])
        return carry

    lax.fori_loop(0, GROUPS, one_group, 0)


def shares_kernel(f0, face_ref, part, acc):
    acc[...] = part[...]

    def one_group(src, carry):
        for k in range(RES):
            scale = scale_of(f0, src, k)
            for z in (OUTER, INNER):
                got = []
                for q in range(2 * RES):
                    o = face_row(k, q, z)
                    got.append(face_ref[src, o:o + ROWS].astype(F32))
                for n, r in enumerate(CORE_ROWS):
                    a = [field(f0, None, None, src, k, c, z, r) * scale for c in range(COMPS)]
                    add_products(acc, z, r - H, a, [t[8 * n:8 * n + 8] for t in got])
        return carry

    lax.fori_loop(0, GROUPS, one_group, 0)


def join_kernel(core_ref, owner_ref, f0, in3_ref, part, out_ref, acc, fi3, blk):
    def get(src, k, c, m, r):
        return field(f0, None, fi3, src, k, c, m, r)

    core = core_ref[0]
    fi3[...] = in3_ref[owner_ref[0] // RES].astype(F32)
    take_block(owner_ref, blk, (IN3,), get)
    for j in range(RES):
        for c in range(COMPS):
            out_ref[j, c, core] = part[j, c, OUTER]
            acc[j, c, 0] = part[j, c, INNER]

    def one_group(src, carry):
        fi3[...] = in3_ref[src].astype(F32)
        for k in range(RES):
            scale = scale_of(f0, src, k)
            for r in CORE_ROWS:
                far = [get(src, k, c, IN3, r) for c in range(COMPS)]
                v = []
                for j in range(RES):
                    v.extend(densities(far, [blk[j, 0, c, r:r + 8] for c in range(COMPS)]))
                a = [get(src, k, c, INNER, r) * scale for c in range(COMPS)]
                add_products(acc, 0, r - H, a, v)
        return carry

    lax.fori_loop(0, GROUPS, one_group, 0)
    for j in range(RES):
        for c in range(COMPS):
            out_ref[j, c, 1 - core] = acc[j, c, 0]


INTERPRET = False
KEEP = True
GRANT = 16 * 1024 * 1024


def on_device(bands, occ_level, block_owner):
    smem = pl.BlockSpec(memory_space=pltpu.SMEM)
    vmem = pl.BlockSpec(memory_space=pltpu.VMEM)
    hbm = pl.BlockSpec(memory_space=pltpu.HBM if KEEP else pl.ANY)

    def made(shape, dtype):
        return pltpu.VMEM(shape, dtype) if KEEP else jax.ShapeDtypeStruct(shape, dtype)

    def kept(value):
        return pltpu.with_memory_space_constraint(value, pltpu.VMEM) if KEEP else value

    def in_hbm(value):
        return pltpu.with_memory_space_constraint(value, pltpu.HBM) if KEEP else value

    def call(kernel, out_shape, in_specs, scratch):
        out_specs = [vmem] * len(out_shape) if isinstance(out_shape, list) else vmem
        return pl.pallas_call(
            kernel, out_shape=out_shape, in_specs=in_specs, out_specs=out_specs,
            scratch_shapes=scratch, interpret=INTERPRET,
            compiler_params=pltpu.CompilerParams(vmem_limit_bytes=GRANT))

    x = bands.shape[3]
    place = lax.axis_index("space").astype(jnp.int32)
    core = (place & 1).reshape(1)
    send = call(
        pack_kernel, made((GROUPS, SEND, LANES), BF16), [smem, hbm, hbm],
        [pltpu.VMEM((RES * COMPS * PLANES, x, LANES), BF16), pltpu.SMEM((RES,), jnp.int32),
         pltpu.VMEM((PLANES * RES * COMPS, x + 16, LANES), F32), pltpu.VMEM((SEND, LANES), F32),
         pltpu.SemaphoreType.DMA((RES * COMPS,)), pltpu.SemaphoreType.DMA],
    )(core, in_hbm(bands.reshape(RES * COMPS * PLANES, x, LANES)), in_hbm(occ_level))
    own = kept(lax.all_to_all(send, "band", 0, 0, tiled=True))

    wide, in1, in3 = call(
        cut_kernel,
        [made((GROUPS, SEND, LANES), F32), made((GROUPS, N1, LANES), BF16), made((GROUPS, N2, LANES), BF16)],
        [vmem], [pltpu.VMEM((N1, LANES), F32), pltpu.VMEM((N2, LANES), F32)],
    )(own)
    wide = kept(wide)
    count = lax.axis_size("space")

    def shift(value, even, odd):
        pairs = [(i, (i + (odd if i % 2 else even)) % count) for i in range(count)]
        value = lax.ppermute(value, "space", pairs)
        return kept(value)

    in1 = shift(in1, 1, -1)

    den, fab = call(
        own_face_kernel,
        [made((GROUPS * RES, 2 * RES, 2, 24, LANES), F32), made((GROUPS, NF, LANES), F32)],
        [smem, vmem],
        [pltpu.VMEM((RES, 2, COMPS, 24, LANES), F32), pltpu.VMEM((RES, 2 * RES, 24, LANES), F32),
         pltpu.VMEM((RES, 2 * RES, 24, LANES), F32)],
    )(block_owner, wide)
    den1, face = call(
        face_kernel,
        [made((GROUPS * RES, 2 * RES, 24, LANES), F32), made((GROUPS, NF, LANES), BF16)],
        [smem] + [vmem] * 2,
        [pltpu.VMEM((N1, LANES), F32), pltpu.VMEM((RES, 1, COMPS, 24, LANES), F32)],
    )(block_owner, kept(fab), in1)
    face = shift(face, -1, 1)

    part = call(
        local_kernel, made((RES, COMPS, PLANES, ROWS, LANES), F32),
        [smem] + [vmem] * 4,
        [pltpu.VMEM((N1, LANES), F32), pltpu.VMEM((RES, 1, COMPS, 24, LANES), F32),
         pltpu.VMEM((2 * RES, 1, 24, LANES), F32)] + [pltpu.VMEM((2 * RES, 2, 24, LANES), F32)] * 2,
    )(block_owner, wide, in1, kept(den), kept(den1))
    in3 = shift(in3, -2, 2)

    part = call(shares_kernel, made((RES, COMPS, PLANES, ROWS, LANES), F32), [vmem] * 3, [])(
        wide, face, kept(part))

    return call(
        join_kernel, jax.ShapeDtypeStruct((RES, COMPS, PLANES, ROWS, LANES), F32),
        [smem, smem] + [vmem] * 3,
        [pltpu.VMEM((RES, COMPS, 1, ROWS, LANES), F32), pltpu.VMEM((N2, LANES), F32),
         pltpu.VMEM((RES, 1, COMPS, 24, LANES), F32)],
    )(core, block_owner, wide, in3, kept(part))


def solution(mesh):
    return jax.shard_map(
        on_device,
        mesh=mesh,
        in_specs=(P("band", None, "space", None, None), P("band"), P()),
        out_specs=P(None, None, "space", "band", None),
        check_vma=False,
    )
```

```python
import jax
import jax.numpy as jnp
from jax import lax
from jax.experimental import pallas as pl
from jax.experimental.pallas import tpu as pltpu
from jax.sharding import PartitionSpec as P


SWEEPS = 4
jacobi_diagonal = 6.5

H = SWEEPS - 1
RES = 2
COMPS = 4
PLANES = 2
LANES = 128
GROUPS = 8
ROWS = 16
WIN = ROWS + 2 * H
BODY = PLANES * RES * COMPS * WIN
SEND = BODY + 8
F32 = jnp.float32
BF16 = jnp.bfloat16


def rows_of(d):
    return d, WIN - d


def plane_row(p, k, c):
    return ((p * RES + k) * COMPS + c) * WIN


N1 = RES * COMPS * ((WIN - 2) + (WIN - 4))
N2 = RES * COMPS * (WIN - 6)
NF = RES * 2 * RES * 2 * ROWS


def near_row(k, c):
    return (k * COMPS + c) * (WIN - 2)


def mid_row(k, c):
    return RES * COMPS * (WIN - 2) + (k * COMPS + c) * (WIN - 4)


def far_row(k, c):
    return (k * COMPS + c) * (WIN - 6)


def face_row(k, q, f):
    return ((k * 2 * RES + q) * 2 + f) * ROWS


OUTER, INNER, IN1, IN2, IN3 = range(5)
D1, D2, D3 = jacobi_diagonal, jacobi_diagonal ** 2, jacobi_diagonal ** 3


def pack_kernel(core_ref, bands_hbm, occ_hbm, out_ref, raw, occ_ref, ext, flat, sems, occ_sem):
    x = raw.shape[1]
    core = core_ref[0]
    levels = pltpu.make_async_copy(occ_hbm, occ_ref, occ_sem)
    levels.start()
    copies = [pltpu.make_async_copy(bands_hbm.at[pl.ds(PLANES * m, PLANES)], raw.at[pl.ds(PLANES * m, PLANES)], sems.at[m])
              for m in range(RES * COMPS)]
    for copy in copies:
        copy.start()
    for m, copy in enumerate(copies):
        copy.wait()
        for p in range(PLANES):
            plane = core if p == 0 else 1 - core
            n = p * RES * COMPS + m
            t = raw[m * PLANES + plane].astype(F32)
            ext[n, 8:8 + x] = t
            ext[n, 0:8] = t[x - 8:x]
            ext[n, 8 + x:16 + x] = t[0:8]
    levels.wait()
    for k in range(RES):
        flat[BODY + 4 * k:BODY + 4 * k + 4] = jnp.full((4, LANES), occ_ref[k].astype(F32), F32)
    for b in range(GROUPS):
        for n in range(PLANES * RES * COMPS):
            flat[n * WIN:(n + 1) * WIN] = ext[n, ROWS * b + 8 - H:ROWS * b + 8 - H + WIN]
        out_ref[b] = flat[...].astype(BF16)


def cut_kernel(own_ref, wide_ref, in1_ref, in3_ref, s1, s4):
    def one(src, carry):
        wide_ref[src] = own_ref[src].astype(F32)
        for k in range(RES):
            for c in range(COMPS):
                a = plane_row(0, k, c)
                o = plane_row(1, k, c)
                q = near_row(k, c)
                s1[q:q + WIN - 2] = wide_ref[src, o + 1:o + WIN - 1]
                q = mid_row(k, c)
                s1[q:q + WIN - 4] = wide_ref[src, a + 2:a + WIN - 2]
                q = far_row(k, c)
                s4[q:q + WIN - 6] = wide_ref[src, a + 3:a + WIN - 3]
        in1_ref[src] = s1[...].astype(BF16)
        in3_ref[src] = s4[...].astype(BF16)
        return carry

    lax.fori_loop(0, GROUPS, one, 0)


def starts_of(lo, hi):
    out = list(range(lo, hi - 7, 8))
    if out[-1] + 8 < hi:
        out.append(hi - 8)
    return out


def span(m):
    return rows_of(max(m - INNER, 0))


CORE_ROWS = starts_of(H, H + ROWS)


def field(f0, fi, fi3, src, k, c, m, r):
    if m in (OUTER, INNER):
        q = plane_row(m, k, c) + r
        return f0[src, q:q + 8]
    if m == IN1:
        q = near_row(k, c) + r - 1
        return fi[q:q + 8]
    if m == IN2:
        q = mid_row(k, c) + r - 2
        return fi[q:q + 8]
    q = far_row(k, c) + r - 3
    return fi3[q:q + 8]


def take_block(owner_ref, blk, planes, get):
    first = owner_ref[0]
    group = first // RES
    swap = (first % RES) == 1
    for i, m in enumerate(planes):
        for r in starts_of(*span(m)):
            for c in range(COMPS):
                b0 = get(group, 0, c, m, r)
                b1 = get(group, 1, c, m, r)
                blk[0, i, c, r:r + 8] = jnp.where(swap, b1, b0)
                blk[1, i, c, r:r + 8] = jnp.where(swap, b0, b1)


def densities(a, b):
    re = (a[0] * b[0] + a[1] * b[1]) + (a[2] * b[2] + a[3] * b[3])
    im = (a[0] * b[1] - a[1] * b[0]) + (a[2] * b[3] - a[3] * b[2])
    return re, im


def turned(t):
    return pltpu.roll(t, 1, 1) + pltpu.roll(t, LANES - 1, 1)


def own_face_body(owner_ref, f0, den, fab, blk, lap, us):
    def get(src, k, c, m, r):
        return field(f0, None, None, src, k, c, m, r)

    planes = (OUTER, INNER)
    take_block(owner_ref, blk, planes, get)

    def one_group(src, carry):
        for k in range(RES):
            i = src * RES + k
            for m in planes:
                for r in starts_of(*span(m)):
                    a = [get(src, k, c, m, r) for c in range(COMPS)]
                    for j in range(RES):
                        re, im = densities(a, [blk[j, m, c, r:r + 8] for c in range(COMPS)])
                        den[i, 2 * j, m, r:r + 8] = re
                        den[i, 2 * j + 1, m, r:r + 8] = im
            for q in range(2 * RES):
                for r in starts_of(2, WIN - 2):
                    e0 = den[i, q, OUTER, r:r + 8]
                    plane = (den[i, q, OUTER, r - 1:r + 7] + den[i, q, OUTER, r + 1:r + 9]) + turned(e0)
                    lap[k, q, r:r + 8] = plane
                    us[k, q, r:r + 8] = (2.0 * D1) * e0 + 3.0 * (den[i, q, INNER, r:r + 8] + plane)
                for n, r in enumerate(CORE_ROWS):
                    e0 = den[i, q, OUTER, r:r + 8]
                    e1 = den[i, q, INNER, r:r + 8]
                    plane = (us[k, q, r - 1:r + 7] + us[k, q, r + 1:r + 9]) + turned(us[k, q, r:r + 8])
                    o = face_row(k, q, 0) + 8 * n
                    fab[src, o:o + 8] = ((D2 + 3.0) * e0 + D1 * e1) + plane
                    o = face_row(k, q, 1) + 8 * n
                    fab[src, o:o + 8] = (D1 * e0 + e1) + 3.0 * lap[k, q, r:r + 8]
        return carry

    lax.fori_loop(0, GROUPS, one_group, 0)


def own_odd_kernel(core_ref, *refs):
    pl.when(core_ref[0] == 1)(lambda: own_face_body(*refs))


def own_even_kernel(core_ref, owner_ref, f0, den_in, fab_in, *refs):
    pl.when(core_ref[0] == 0)(lambda: own_face_body(owner_ref, f0, *refs))


def face_kernel(owner_ref, fab, in1_ref, den1, face_ref, fi, blk):
    def get(src, k, c, m, r):
        return field(None, fi, None, src, k, c, m, r)

    fi[...] = in1_ref[owner_ref[0] // RES].astype(F32)
    take_block(owner_ref, blk, (IN1,), get)

    def one_group(src, carry):
        near = RES * COMPS * (WIN - 2)
        fi[0:near] = in1_ref[src, 0:near].astype(F32)
        for k in range(RES):
            i = src * RES + k
            for r in starts_of(*span(IN1)):
                a = [get(src, k, c, IN1, r) for c in range(COMPS)]
                for j in range(RES):
                    re, im = densities(a, [blk[j, 0, c, r:r + 8] for c in range(COMPS)])
                    den1[i, 2 * j, r:r + 8] = re
                    den1[i, 2 * j + 1, r:r + 8] = im
            for q in range(2 * RES):
                o = face_row(k, q, 0)
                face_ref[src, o:o + ROWS] = (fab[src, o:o + ROWS] + den1[i, q, H:H + ROWS]).astype(BF16)
                o = face_row(k, q, 1)
                face_ref[src, o:o + ROWS] = fab[src, o:o + ROWS].astype(BF16)
        return carry

    lax.fori_loop(0, GROUPS, one_group, 0)


def scale_of(f0, src, k):
    level = f0[src, BODY + 4 * k:BODY + 4 * k + 1]
    return jnp.broadcast_to(level * (-0.25 * 0.25 / jacobi_diagonal ** 4), (8, LANES))


def add_products(out_ref, p, o, a, v):
    for j in range(RES):
        re, im = v[2 * j], v[2 * j + 1]
        for s in range(2):
            out_ref[j, 2 * s, p, o:o + 8] += a[2 * s] * re - a[2 * s + 1] * im
            out_ref[j, 2 * s + 1, p, o:o + 8] += a[2 * s] * im + a[2 * s + 1] * re


def local_kernel(owner_ref, f0, in1_ref, den, den1, out_ref, fi, blk, d2s, t2s, t1s):
    def get(src, k, c, m, r):
        return field(f0, fi, None, src, k, c, m, r)

    def widen(src):
        fi[...] = in1_ref[src].astype(F32)

    planes = (IN2,)
    widen(owner_ref[0] // RES)
    take_block(owner_ref, blk, planes, get)
    out_ref[...] = jnp.zeros(out_ref.shape, F32)
    mids = starts_of(1, WIN - 1)

    def one_group(src, carry):
        widen(src)
        for k in range(RES):
            i = src * RES + k
            for z, m in enumerate(planes):
                for r in starts_of(*span(m)):
                    a = [get(src, k, c, m, r) for c in range(COMPS)]
                    for j in range(RES):
                        re, im = densities(a, [blk[j, z, c, r:r + 8] for c in range(COMPS)])
                        d2s[2 * j, z, r:r + 8] = re
                        d2s[2 * j + 1, z, r:r + 8] = im
            scale = scale_of(f0, src, k)

            def at(q, m, r):
                if m == IN2:
                    return d2s[q, 0, r:r + 8]
                if m == IN1:
                    return den1[i, q, r:r + 8]
                return den[i, q, m, r:r + 8]

            def pair(q, z, d, r):
                t = at(q, z + d, r)
                return t + at(q, z - d, r) if z - d >= OUTER else t

            for z in (OUTER, INNER):
                t0 = {}
                for q in range(2 * RES):
                    kept = []
                    for r in mids:
                        e0 = at(q, z, r)
                        e1 = pair(q, z, 1, r)
                        e2 = pair(q, z, 2, r)
                        plane = (at(q, z, r - 1) + at(q, z, r + 1)) + turned(e0)
                        t2 = (D1 * e0 + 3.0 * e1) + plane
                        t2s[q, z, r:r + 8] = t2
                        kept.append((t2, ((D2 + 6.0) * e0 + (2.0 * D1) * e1) + 3.0 * e2))
                    for r, (t2, a1) in zip(mids, kept):
                        plane = (t2s[q, z, r - 1:r + 7] + t2s[q, z, r + 1:r + 9]) + turned(t2)
                        t1s[q, z, r:r + 8] = a1 + plane
                    for r in CORE_ROWS:
                        a0 = ((D3 + 2.0 * D1) * at(q, z, r) + (D2 + 3.0) * pair(q, z, 1, r)) + D1 * pair(q, z, 2, r)
                        if z + 3 <= IN2:
                            a0 = a0 + at(q, z + 3, r)
                        plane = (t1s[q, z, r - 1:r + 7] + t1s[q, z, r + 1:r + 9]) + turned(t1s[q, z, r:r + 8])
                        t0[q, r] = scale * (a0 + plane)
                for r in CORE_ROWS:
                    a = [get(src, k, c, z, r) for c in range(COMPS)]
                    add_products(out_ref, z, r - H, a, [t0[q, r] for q in range(2 * RES)])
        return carry

    lax.fori_loop(0, GROUPS, one_group, 0)


def shares_kernel(f0, face_ref, part, acc):
    acc[...] = part[...]

    def one_group(src, carry):
        for k in range(RES):
            scale = scale_of(f0, src, k)
            for z in (OUTER, INNER):
                got = []
                for q in range(2 * RES):
                    o = face_row(k, q, z)
                    got.append(face_ref[src, o:o + ROWS].astype(F32))
                for n, r in enumerate(CORE_ROWS):
                    a = [field(f0, None, None, src, k, c, z, r) * scale for c in range(COMPS)]
                    add_products(acc, z, r - H, a, [t[8 * n:8 * n + 8] for t in got])
        return carry

    lax.fori_loop(0, GROUPS, one_group, 0)


def join_kernel(core_ref, owner_ref, f0, in3_ref, part, out_ref, acc, fi3, blk):
    def get(src, k, c, m, r):
        return field(f0, None, fi3, src, k, c, m, r)

    core = core_ref[0]
    fi3[...] = in3_ref[owner_ref[0] // RES].astype(F32)
    take_block(owner_ref, blk, (IN3,), get)
    for j in range(RES):
        for c in range(COMPS):
            out_ref[j, c, core] = part[j, c, OUTER]
            acc[j, c, 0] = part[j, c, INNER]

    def one_group(src, carry):
        fi3[...] = in3_ref[src].astype(F32)
        for k in range(RES):
            scale = scale_of(f0, src, k)
            for r in CORE_ROWS:
                far = [get(src, k, c, IN3, r) for c in range(COMPS)]
                v = []
                for j in range(RES):
                    v.extend(densities(far, [blk[j, 0, c, r:r + 8] for c in range(COMPS)]))
                a = [get(src, k, c, INNER, r) * scale for c in range(COMPS)]
                add_products(acc, 0, r - H, a, v)
        return carry

    lax.fori_loop(0, GROUPS, one_group, 0)
    for j in range(RES):
        for c in range(COMPS):
            out_ref[j, c, 1 - core] = acc[j, c, 0]


INTERPRET = False
KEEP = True
GRANT = 16 * 1024 * 1024


def on_device(bands, occ_level, block_owner):
    smem = pl.BlockSpec(memory_space=pltpu.SMEM)
    vmem = pl.BlockSpec(memory_space=pltpu.VMEM)
    hbm = pl.BlockSpec(memory_space=pltpu.HBM if KEEP else pl.ANY)

    def made(shape, dtype):
        return pltpu.VMEM(shape, dtype) if KEEP else jax.ShapeDtypeStruct(shape, dtype)

    def kept(value):
        return pltpu.with_memory_space_constraint(value, pltpu.VMEM) if KEEP else value

    def in_hbm(value):
        return pltpu.with_memory_space_constraint(value, pltpu.HBM) if KEEP else value

    def call(kernel, out_shape, in_specs, scratch, aliases={}):
        out_specs = [vmem] * len(out_shape) if isinstance(out_shape, list) else vmem
        return pl.pallas_call(
            kernel, out_shape=out_shape, in_specs=in_specs, out_specs=out_specs,
            scratch_shapes=scratch, interpret=INTERPRET, input_output_aliases=aliases,
            compiler_params=pltpu.CompilerParams(vmem_limit_bytes=GRANT))

    x = bands.shape[3]
    place = lax.axis_index("space").astype(jnp.int32)
    core = (place & 1).reshape(1)
    send = call(
        pack_kernel, made((GROUPS, SEND, LANES), BF16), [smem, hbm, hbm],
        [pltpu.VMEM((RES * COMPS * PLANES, x, LANES), BF16), pltpu.SMEM((RES,), jnp.int32),
         pltpu.VMEM((PLANES * RES * COMPS, x + 16, LANES), F32), pltpu.VMEM((SEND, LANES), F32),
         pltpu.SemaphoreType.DMA((RES * COMPS,)), pltpu.SemaphoreType.DMA],
    )(core, in_hbm(bands.reshape(RES * COMPS * PLANES, x, LANES)), in_hbm(occ_level))
    own = kept(lax.all_to_all(send, "band", 0, 0, tiled=True))

    wide, in1, in3 = call(
        cut_kernel,
        [made((GROUPS, SEND, LANES), F32), made((GROUPS, N1, LANES), BF16), made((GROUPS, N2, LANES), BF16)],
        [vmem], [pltpu.VMEM((N1, LANES), F32), pltpu.VMEM((N2, LANES), F32)],
    )(own)
    wide = kept(wide)
    count = lax.axis_size("space")

    def shift(value, even, odd):
        pairs = [(i, (i + (odd if i % 2 else even)) % count) for i in range(count)]
        value = lax.ppermute(value, "space", pairs)
        return kept(value)

    in1 = shift(in1, 1, -1)

    own_out = [made((GROUPS * RES, 2 * RES, 2, 24, LANES), F32), made((GROUPS, NF, LANES), F32)]
    own_scratch = [pltpu.VMEM((RES, 2, COMPS, 24, LANES), F32), pltpu.VMEM((RES, 2 * RES, 24, LANES), F32),
                   pltpu.VMEM((RES, 2 * RES, 24, LANES), F32)]
    den, fab = call(own_odd_kernel, own_out, [smem, smem, vmem],
                    own_scratch)(core, block_owner, wide)
    den, fab = call(own_even_kernel, own_out, [smem, smem] + [vmem] * 3,
                    own_scratch, {3: 0, 4: 1})(core, block_owner, wide, kept(den), kept(fab))
    den1, face = call(
        face_kernel,
        [made((GROUPS * RES, 2 * RES, 24, LANES), F32), made((GROUPS, NF, LANES), BF16)],
        [smem] + [vmem] * 2,
        [pltpu.VMEM((N1, LANES), F32), pltpu.VMEM((RES, 1, COMPS, 24, LANES), F32)],
    )(block_owner, kept(fab), in1)
    face = shift(face, -1, 1)

    part = call(
        local_kernel, made((RES, COMPS, PLANES, ROWS, LANES), F32),
        [smem] + [vmem] * 4,
        [pltpu.VMEM((N1, LANES), F32), pltpu.VMEM((RES, 1, COMPS, 24, LANES), F32),
         pltpu.VMEM((2 * RES, 1, 24, LANES), F32)] + [pltpu.VMEM((2 * RES, 2, 24, LANES), F32)] * 2,
    )(block_owner, wide, in1, kept(den), kept(den1))
    in3 = shift(in3, -2, 2)

    part = call(shares_kernel, made((RES, COMPS, PLANES, ROWS, LANES), F32), [vmem] * 3, [])(
        wide, face, kept(part))

    return call(
        join_kernel, jax.ShapeDtypeStruct((RES, COMPS, PLANES, ROWS, LANES), F32),
        [smem, smem] + [vmem] * 3,
        [pltpu.VMEM((RES, COMPS, 1, ROWS, LANES), F32), pltpu.VMEM((N2, LANES), F32),
         pltpu.VMEM((RES, 1, COMPS, 24, LANES), F32)],
    )(core, block_owner, wide, in3, kept(part))


def solution(mesh):
    return jax.shard_map(
        on_device,
        mesh=mesh,
        in_specs=(P("band", None, "space", None, None), P("band"), P()),
        out_specs=P(None, None, "space", "band", None),
        check_vma=False,
    )
```

```python
import jax
import jax.numpy as jnp
from jax import lax
from jax.experimental import pallas as pl
from jax.experimental.pallas import tpu as pltpu
from jax.sharding import PartitionSpec as P


SWEEPS = 4
jacobi_diagonal = 6.5

H = SWEEPS - 1
RES = 2
COMPS = 4
PLANES = 2
LANES = 128
GROUPS = 8
ROWS = 16
WIN = ROWS + 2 * H
BODY = PLANES * RES * COMPS * WIN
SEND = BODY + 8
F32 = jnp.float32
BF16 = jnp.bfloat16


def rows_of(d):
    return d, WIN - d


def plane_row(p, k, c):
    return ((p * RES + k) * COMPS + c) * WIN


N1 = RES * COMPS * ((WIN - 2) + (WIN - 4))
N2 = RES * COMPS * (WIN - 6)
NF = RES * 2 * RES * 2 * ROWS


def near_row(k, c):
    return (k * COMPS + c) * (WIN - 2)


def mid_row(k, c):
    return RES * COMPS * (WIN - 2) + (k * COMPS + c) * (WIN - 4)


def far_row(k, c):
    return (k * COMPS + c) * (WIN - 6)


def face_row(k, q, f):
    return ((k * 2 * RES + q) * 2 + f) * ROWS


OUTER, INNER, IN1, IN2, IN3 = range(5)
D1, D2, D3 = jacobi_diagonal, jacobi_diagonal ** 2, jacobi_diagonal ** 3


def pack_kernel(core_ref, bands_hbm, occ_hbm, out_ref, raw, occ_ref, ext, flat, sems, occ_sem):
    x = raw.shape[1]
    core = core_ref[0]
    levels = pltpu.make_async_copy(occ_hbm, occ_ref, occ_sem)
    levels.start()
    copies = [pltpu.make_async_copy(bands_hbm.at[pl.ds(PLANES * m, PLANES)], raw.at[pl.ds(PLANES * m, PLANES)], sems.at[m])
              for m in range(RES * COMPS)]
    for copy in copies:
        copy.start()
    for m, copy in enumerate(copies):
        copy.wait()
        for p in range(PLANES):
            plane = core if p == 0 else 1 - core
            n = p * RES * COMPS + m
            t = raw[m * PLANES + plane].astype(F32)
            ext[n, 8:8 + x] = t
            ext[n, 0:8] = t[x - 8:x]
            ext[n, 8 + x:16 + x] = t[0:8]
    levels.wait()
    for b in range(GROUPS):
        for k in range(RES):
            flat[b, BODY + 4 * k:BODY + 4 * k + 4] = jnp.full((4, LANES), occ_ref[k].astype(F32), F32)
        for n in range(PLANES * RES * COMPS):
            flat[b, n * WIN:(n + 1) * WIN] = ext[n, ROWS * b + 8 - H:ROWS * b + 8 - H + WIN]
        out_ref[b] = flat[b].astype(BF16)


def cut_kernel(own_ref, wide_ref, in1_ref, in3_ref, s1, s4):
    def one(src, carry):
        wide_ref[src] = own_ref[src].astype(F32)
        for k in range(RES):
            for c in range(COMPS):
                a = plane_row(0, k, c)
                o = plane_row(1, k, c)
                q = near_row(k, c)
                s1[q:q + WIN - 2] = wide_ref[src, o + 1:o + WIN - 1]
                q = mid_row(k, c)
                s1[q:q + WIN - 4] = wide_ref[src, a + 2:a + WIN - 2]
                q = far_row(k, c)
                s4[q:q + WIN - 6] = wide_ref[src, a + 3:a + WIN - 3]
        in1_ref[src] = s1[...].astype(BF16)
        in3_ref[src] = s4[...].astype(BF16)
        return carry

    lax.fori_loop(0, GROUPS, one, 0)


def starts_of(lo, hi):
    out = list(range(lo, hi - 7, 8))
    if out[-1] + 8 < hi:
        out.append(hi - 8)
    return out


def span(m):
    return rows_of(max(m - INNER, 0))


CORE_ROWS = starts_of(H, H + ROWS)


def field(f0, fi, fi3, src, k, c, m, r):
    if m in (OUTER, INNER):
        q = plane_row(m, k, c) + r
        return f0[src, q:q + 8]
    if m == IN1:
        q = near_row(k, c) + r - 1
        return fi[q:q + 8]
    if m == IN2:
        q = mid_row(k, c) + r - 2
        return fi[q:q + 8]
    q = far_row(k, c) + r - 3
    return fi3[q:q + 8]


def take_block(owner_ref, blk, planes, get):
    first = owner_ref[0]
    group = first // RES
    swap = (first % RES) == 1
    for i, m in enumerate(planes):
        for r in starts_of(*span(m)):
            for c in range(COMPS):
                b0 = get(group, 0, c, m, r)
                b1 = get(group, 1, c, m, r)
                blk[0, i, c, r:r + 8] = jnp.where(swap, b1, b0)
                blk[1, i, c, r:r + 8] = jnp.where(swap, b0, b1)


def densities(a, b):
    re = (a[0] * b[0] + a[1] * b[1]) + (a[2] * b[2] + a[3] * b[3])
    im = (a[0] * b[1] - a[1] * b[0]) + (a[2] * b[3] - a[3] * b[2])
    return re, im


def turned(t):
    return pltpu.roll(t, 1, 1) + pltpu.roll(t, LANES - 1, 1)


def own_face_kernel(owner_ref, f0, den, fab, blk, lap, us):
    def get(src, k, c, m, r):
        return field(f0, None, None, src, k, c, m, r)

    planes = (OUTER, INNER)
    take_block(owner_ref, blk, planes, get)

    def one_group(src, carry):
        for k in range(RES):
            i = src * RES + k
            for m in planes:
                for r in starts_of(*span(m)):
                    a = [get(src, k, c, m, r) for c in range(COMPS)]
                    for j in range(RES):
                        re, im = densities(a, [blk[j, m, c, r:r + 8] for c in range(COMPS)])
                        den[i, 2 * j, m, r:r + 8] = re
                        den[i, 2 * j + 1, m, r:r + 8] = im
            for q in range(2 * RES):
                for r in starts_of(2, WIN - 2):
                    e0 = den[i, q, OUTER, r:r + 8]
                    plane = (den[i, q, OUTER, r - 1:r + 7] + den[i, q, OUTER, r + 1:r + 9]) + turned(e0)
                    lap[k, q, r:r + 8] = plane
                    us[k, q, r:r + 8] = (2.0 * D1) * e0 + 3.0 * (den[i, q, INNER, r:r + 8] + plane)
                for n, r in enumerate(CORE_ROWS):
                    e0 = den[i, q, OUTER, r:r + 8]
                    e1 = den[i, q, INNER, r:r + 8]
                    plane = (us[k, q, r - 1:r + 7] + us[k, q, r + 1:r + 9]) + turned(us[k, q, r:r + 8])
                    o = face_row(k, q, 0) + 8 * n
                    fab[src, o:o + 8] = ((D2 + 3.0) * e0 + D1 * e1) + plane
                    o = face_row(k, q, 1) + 8 * n
                    fab[src, o:o + 8] = (D1 * e0 + e1) + 3.0 * lap[k, q, r:r + 8]
        return carry

    lax.fori_loop(0, GROUPS, one_group, 0)


def face_kernel(owner_ref, fab, in1_ref, den1, face_ref, fi, blk):
    def get(src, k, c, m, r):
        return field(None, fi, None, src, k, c, m, r)

    fi[...] = in1_ref[owner_ref[0] // RES].astype(F32)
    take_block(owner_ref, blk, (IN1,), get)

    def one_group(src, carry):
        near = RES * COMPS * (WIN - 2)
        fi[0:near] = in1_ref[src, 0:near].astype(F32)
        for k in range(RES):
            i = src * RES + k
            for r in starts_of(*span(IN1)):
                a = [get(src, k, c, IN1, r) for c in range(COMPS)]
                for j in range(RES):
                    re, im = densities(a, [blk[j, 0, c, r:r + 8] for c in range(COMPS)])
                    den1[i, 2 * j, r:r + 8] = re
                    den1[i, 2 * j + 1, r:r + 8] = im
            for q in range(2 * RES):
                o = face_row(k, q, 0)
                face_ref[src, o:o + ROWS] = (fab[src, o:o + ROWS] + den1[i, q, H:H + ROWS]).astype(BF16)
                o = face_row(k, q, 1)
                face_ref[src, o:o + ROWS] = fab[src, o:o + ROWS].astype(BF16)
        return carry

    lax.fori_loop(0, GROUPS, one_group, 0)


def scale_of(f0, src, k):
    level = f0[src, BODY + 4 * k:BODY + 4 * k + 1]
    return jnp.broadcast_to(level * (-0.25 * 0.25 / jacobi_diagonal ** 4), (8, LANES))


def add_products(out_ref, p, o, a, v):
    for j in range(RES):
        re, im = v[2 * j], v[2 * j + 1]
        for s in range(2):
            out_ref[j, 2 * s, p, o:o + 8] += a[2 * s] * re - a[2 * s + 1] * im
            out_ref[j, 2 * s + 1, p, o:o + 8] += a[2 * s] * im + a[2 * s + 1] * re


def local_kernel(owner_ref, f0, in1_ref, den, den1, out_ref, fi, blk, d2s, t2s, t1s):
    def get(src, k, c, m, r):
        return field(f0, fi, None, src, k, c, m, r)

    def widen(src):
        near = mid_row(0, 0)
        fi[near:N1] = in1_ref[src, near:N1].astype(F32)

    planes = (IN2,)
    widen(owner_ref[0] // RES)
    take_block(owner_ref, blk, planes, get)
    out_ref[...] = jnp.zeros(out_ref.shape, F32)
    mids = starts_of(1, WIN - 1)

    def one_group(src, carry):
        widen(src)
        for k in range(RES):
            i = src * RES + k
            for z, m in enumerate(planes):
                for r in starts_of(*span(m)):
                    a = [get(src, k, c, m, r) for c in range(COMPS)]
                    for j in range(RES):
                        re, im = densities(a, [blk[j, z, c, r:r + 8] for c in range(COMPS)])
                        d2s[2 * j, z, r:r + 8] = re
                        d2s[2 * j + 1, z, r:r + 8] = im
            scale = scale_of(f0, src, k)

            def at(q, m, r):
                if m == IN2:
                    return d2s[q, 0, r:r + 8]
                if m == IN1:
                    return den1[i, q, r:r + 8]
                return den[i, q, m, r:r + 8]

            def pair(q, z, d, r):
                t = at(q, z + d, r)
                return t + at(q, z - d, r) if z - d >= OUTER else t

            for z in (OUTER, INNER):
                t0 = {}
                for q in range(2 * RES):
                    kept = []
                    for r in mids:
                        e0 = at(q, z, r)
                        e1 = pair(q, z, 1, r)
                        e2 = pair(q, z, 2, r)
                        plane = (at(q, z, r - 1) + at(q, z, r + 1)) + turned(e0)
                        t2 = (D1 * e0 + 3.0 * e1) + plane
                        t2s[q, z, r:r + 8] = t2
                        kept.append((t2, ((D2 + 6.0) * e0 + (2.0 * D1) * e1) + 3.0 * e2))
                    for r, (t2, a1) in zip(mids, kept):
                        plane = (t2s[q, z, r - 1:r + 7] + t2s[q, z, r + 1:r + 9]) + turned(t2)
                        t1s[q, z, r:r + 8] = a1 + plane
                    for r in CORE_ROWS:
                        a0 = ((D3 + 2.0 * D1) * at(q, z, r) + (D2 + 3.0) * pair(q, z, 1, r)) + D1 * pair(q, z, 2, r)
                        if z + 3 <= IN2:
                            a0 = a0 + at(q, z + 3, r)
                        plane = (t1s[q, z, r - 1:r + 7] + t1s[q, z, r + 1:r + 9]) + turned(t1s[q, z, r:r + 8])
                        t0[q, r] = scale * (a0 + plane)
                for r in CORE_ROWS:
                    a = [get(src, k, c, z, r) for c in range(COMPS)]
                    add_products(out_ref, z, r - H, a, [t0[q, r] for q in range(2 * RES)])
        return carry

    lax.fori_loop(0, GROUPS, one_group, 0)


def shares_kernel(f0, face_ref, part, acc):
    acc[...] = part[...]

    def one_group(src, carry):
        for k in range(RES):
            scale = scale_of(f0, src, k)
            for z in (OUTER, INNER):
                got = []
                for q in range(2 * RES):
                    o = face_row(k, q, z)
                    got.append(face_ref[src, o:o + ROWS].astype(F32))
                for n, r in enumerate(CORE_ROWS):
                    a = [field(f0, None, None, src, k, c, z, r) * scale for c in range(COMPS)]
                    add_products(acc, z, r - H, a, [t[8 * n:8 * n + 8] for t in got])
        return carry

    lax.fori_loop(0, GROUPS, one_group, 0)


def join_kernel(core_ref, owner_ref, f0, in3_ref, part, out_ref, acc, fi3, blk):
    def get(src, k, c, m, r):
        return field(f0, None, fi3, src, k, c, m, r)

    core = core_ref[0]
    fi3[...] = in3_ref[owner_ref[0] // RES].astype(F32)
    take_block(owner_ref, blk, (IN3,), get)
    for j in range(RES):
        for c in range(COMPS):
            out_ref[j, c, core] = part[j, c, OUTER]
            acc[j, c, 0] = part[j, c, INNER]

    def one_group(src, carry):
        fi3[...] = in3_ref[src].astype(F32)
        for k in range(RES):
            scale = scale_of(f0, src, k)
            for r in CORE_ROWS:
                far = [get(src, k, c, IN3, r) for c in range(COMPS)]
                v = []
                for j in range(RES):
                    v.extend(densities(far, [blk[j, 0, c, r:r + 8] for c in range(COMPS)]))
                a = [get(src, k, c, INNER, r) * scale for c in range(COMPS)]
                add_products(acc, 0, r - H, a, v)
        return carry

    lax.fori_loop(0, GROUPS, one_group, 0)
    for j in range(RES):
        for c in range(COMPS):
            out_ref[j, c, 1 - core] = acc[j, c, 0]


INTERPRET = False
KEEP = True
GRANT = 16 * 1024 * 1024


def on_device(bands, occ_level, block_owner):
    smem = pl.BlockSpec(memory_space=pltpu.SMEM)
    vmem = pl.BlockSpec(memory_space=pltpu.VMEM)
    hbm = pl.BlockSpec(memory_space=pltpu.HBM if KEEP else pl.ANY)

    def made(shape, dtype):
        return pltpu.VMEM(shape, dtype) if KEEP else jax.ShapeDtypeStruct(shape, dtype)

    def kept(value):
        return pltpu.with_memory_space_constraint(value, pltpu.VMEM) if KEEP else value

    def in_hbm(value):
        return pltpu.with_memory_space_constraint(value, pltpu.HBM) if KEEP else value

    def call(kernel, out_shape, in_specs, scratch):
        out_specs = [vmem] * len(out_shape) if isinstance(out_shape, list) else vmem
        return pl.pallas_call(
            kernel, out_shape=out_shape, in_specs=in_specs, out_specs=out_specs,
            scratch_shapes=scratch, interpret=INTERPRET,
            compiler_params=pltpu.CompilerParams(vmem_limit_bytes=GRANT))

    x = bands.shape[3]
    place = lax.axis_index("space").astype(jnp.int32)
    core = (place & 1).reshape(1)
    send = call(
        pack_kernel, made((GROUPS, SEND, LANES), BF16), [smem, hbm, hbm],
        [pltpu.VMEM((RES * COMPS * PLANES, x, LANES), BF16), pltpu.SMEM((RES,), jnp.int32),
         pltpu.VMEM((PLANES * RES * COMPS, x + 16, LANES), F32), pltpu.VMEM((GROUPS, SEND, LANES), F32),
         pltpu.SemaphoreType.DMA((RES * COMPS,)), pltpu.SemaphoreType.DMA],
    )(core, in_hbm(bands.reshape(RES * COMPS * PLANES, x, LANES)), in_hbm(occ_level))
    own = kept(lax.all_to_all(send, "band", 0, 0, tiled=True))

    wide, in1, in3 = call(
        cut_kernel,
        [made((GROUPS, SEND, LANES), F32), made((GROUPS, N1, LANES), BF16), made((GROUPS, N2, LANES), BF16)],
        [vmem], [pltpu.VMEM((N1, LANES), F32), pltpu.VMEM((N2, LANES), F32)],
    )(own)
    wide = kept(wide)
    count = lax.axis_size("space")

    def shift(value, even, odd):
        pairs = [(i, (i + (odd if i % 2 else even)) % count) for i in range(count)]
        value = lax.ppermute(value, "space", pairs)
        return kept(value)

    in1 = shift(in1, 1, -1)

    den, fab = call(
        own_face_kernel,
        [made((GROUPS * RES, 2 * RES, 2, 24, LANES), F32), made((GROUPS, NF, LANES), F32)],
        [smem, vmem],
        [pltpu.VMEM((RES, 2, COMPS, 24, LANES), F32), pltpu.VMEM((RES, 2 * RES, 24, LANES), F32),
         pltpu.VMEM((RES, 2 * RES, 24, LANES), F32)],
    )(block_owner, wide)
    den1, face = call(
        face_kernel,
        [made((GROUPS * RES, 2 * RES, 24, LANES), F32), made((GROUPS, NF, LANES), BF16)],
        [smem] + [vmem] * 2,
        [pltpu.VMEM((N1, LANES), F32), pltpu.VMEM((RES, 1, COMPS, 24, LANES), F32)],
    )(block_owner, kept(fab), in1)
    face = shift(face, -1, 1)

    part = call(
        local_kernel, made((RES, COMPS, PLANES, ROWS, LANES), F32),
        [smem] + [vmem] * 4,
        [pltpu.VMEM((N1, LANES), F32), pltpu.VMEM((RES, 1, COMPS, 24, LANES), F32),
         pltpu.VMEM((2 * RES, 1, 24, LANES), F32)] + [pltpu.VMEM((2 * RES, 2, 24, LANES), F32)] * 2,
    )(block_owner, wide, in1, kept(den), kept(den1))
    in3 = shift(in3, -2, 2)

    part = call(shares_kernel, made((RES, COMPS, PLANES, ROWS, LANES), F32), [vmem] * 3, [])(
        wide, face, kept(part))

    return call(
        join_kernel, jax.ShapeDtypeStruct((RES, COMPS, PLANES, ROWS, LANES), F32),
        [smem, smem] + [vmem] * 3,
        [pltpu.VMEM((RES, COMPS, 1, ROWS, LANES), F32), pltpu.VMEM((N2, LANES), F32),
         pltpu.VMEM((RES, 1, COMPS, 24, LANES), F32)],
    )(core, block_owner, wide, in3, kept(part))


def solution(mesh):
    return jax.shard_map(
        on_device,
        mesh=mesh,
        in_specs=(P("band", None, "space", None, None), P("band"), P()),
        out_specs=P(None, None, "space", "band", None),
        check_vma=False,
    )
```
